128 devices in a mesh: freq: 4 (over z_lo, core), facet: 32 (over y, x, z_hi).
Axes of the slice: x: 4, y: 4, z: 4 (z_hi: 2, z_lo: 2; z = z_hi * 2 + z_lo), core: 2. Of those that a mesh axis runs over, the one named last changes fastest.
Arguments:
- visibilities: float32 [64, 2, 2048], P('facet', None, 'freq'), may hold values from -6 to 6
- weights: float32 [64, 2048], P('facet', 'freq'), may hold values from 0.1 to 1
- uv_cells: int32 [64, 2, 2048], P('facet', None, 'freq'), may hold values from -16384 to 16383
- flags: int32 [64, 2048], P('facet', 'freq'), may hold values from 0 to 1, as said below
- plan: int32 [64], replicated, may hold values from 0 to 63, each once
- beam: float32 [32, 64], P('facet'), may hold values from 0.2 to 1
- facets: int32 [32, 2], P('facet'), may hold values from 0 to 255
Outputs:
- dirty_image: float32 [32, 128, 128], P('facet', 'freq')
The draws below stay inside these ranges and needn't reach their ends.
Inputs may be any that keep to these rules, and one draw needn't show every extreme that they name: `flags`: in each block, each frequency group's 512 rows hold at most 256 unflagged rows; in every draw some block holds exactly 256 in every group. `plan`: each of the 64 blocks is read at exactly one step.
All inputs are finite; a program needn't handle non-finite values.
Results may differ from the reference program's by a relative error of at most 0.0037.
Values sent between devices are 32-bit elements; how exact they have to be, the bound alone decides.
No kernel may reach another device: no remote copies, remote signals or barrier semaphores. Data moves between devices by JAX's collectives and lax.ppermute only.
A program may use at most 64 MiB of HBM per device.

```python
import math
import jax
import jax.numpy as jnp
from jax import lax

P_SIZE = 128
IMG = 32768
KROWS = 512
KEEP = 256
NBLK = 64
KTOT = 2048
N_FACET = 32


def draw_flags(key, part):
    first_key, second_key, third_key = jax.random.split(key, 3)
    groups = KTOT // KROWS
    dropped = jax.random.randint(first_key, (NBLK, groups), 0, KEEP // 2 + 1)
    chosen = jax.random.randint(second_key, (), 0, NBLK)
    dropped = jnp.where(jnp.arange(NBLK)[:, None] == chosen, 0, dropped)
    counts_live = KEEP - dropped
    key_list = jax.random.split(third_key, NBLK * groups)
    ranking = jax.vmap(lambda single: jax.random.permutation(single, KROWS))(key_list)
    ranking = ranking.reshape(NBLK, groups, KROWS)
    return (ranking < counts_live[:, :, None]).astype(jnp.int32).reshape(NBLK, KTOT)


def plant(values, rng, low, high):
    spot = [jax.random.randint(jax.random.fold_in(rng, axis), (), 0, length) for axis, length in enumerate(values.shape)]
    widest = values.shape.index(max(values.shape))
    neighbour = spot[:widest] + [(spot[widest] + 1) % values.shape[widest]] + spot[widest + 1:]
    return values.at[tuple(spot)].set(low).at[tuple(neighbour)].set(high)


def steps_of(own_key, extent, cuts, least, largest):
    def one(axis_at, shards_of):
        steps = jax.random.uniform(jax.random.fold_in(jax.random.fold_in(own_key, 6), axis_at), (shards_of,), jnp.float32, least / len(cuts), largest / len(cuts))
        return jnp.repeat(jnp.exp(steps), extent[axis_at] // shards_of).reshape((-1,) + (1,) * (len(extent) - axis_at - 1))

    factor_of = one(*cuts[0])
    for cut in cuts[1:]:
        factor_of = factor_of * one(*cut)
    return factor_of


def centred(key, dims, spread, most, cuts=(), held_as=jnp.bfloat16):
    factor_of = steps_of(key, dims, cuts, -0.22, 0.18) if cuts else 1.0
    entries = jax.random.normal(key, dims, jnp.float32) * spread * factor_of
    return jnp.minimum(jnp.maximum(entries, -most), most).astype(held_as)


def setup_inputs(seed: int = 0) -> dict:
    keys = jax.random.split(jax.random.key(seed), 8)
    visibilities = centred(keys[0], (NBLK, 2, KTOT), 1.0, 6.0, ((0, 32), (2, 4)), jnp.float32)
    weights = jnp.clip(jnp.exp(math.log(1.0) - 2.3025851 * jax.random.uniform(keys[1], (NBLK, KTOT), jnp.float32) ** steps_of(keys[1], (NBLK, KTOT), ((0, 32), (1, 4)), -0.2, 0.2)), 0.1, 1.0)
    uv_cells = plant(jax.random.randint(keys[2], (NBLK, 2, KTOT), 0 - IMG // 2, IMG // 2), jax.random.fold_in(keys[2], 1), 0 - IMG // 2, (IMG // 2) - 1).astype(jnp.int32)
    flags = draw_flags(jax.random.fold_in(keys[7], 71), 0)
    plan = jax.random.permutation(keys[4], NBLK).astype(jnp.int32)
    beam = jnp.clip(jnp.exp(math.log(1.0) - 1.609438 * jax.random.uniform(keys[5], (N_FACET, NBLK), jnp.float32) ** steps_of(keys[5], (N_FACET, NBLK), ((0, 32),), -0.2, 0.2)), 0.2, 1.0)
    facets = plant(jax.random.randint(keys[6], (N_FACET, 2), 0, IMG // P_SIZE), jax.random.fold_in(keys[6], 1), 0, (IMG // P_SIZE) - 1).astype(jnp.int32)
    return {"visibilities": visibilities, "weights": weights, "uv_cells": uv_cells, "flags": flags, "plan": plan, "beam": beam, "facets": facets}


full_turn = 2.0 * math.pi

def facet_image(samples, facet_col, facet_row):
    pixels = jnp.arange(P_SIZE, dtype=jnp.int32)
    along_l = (facet_col * P_SIZE + pixels - IMG // 2).astype(jnp.int32)
    along_m = (facet_row * P_SIZE + pixels - IMG // 2).astype(jnp.int32)
    u_cells = samples[3].astype(jnp.int32)
    v_cells = samples[4].astype(jnp.int32)
    turn_u = jnp.mod(along_l[:, None] * u_cells[None, :], IMG).astype(jnp.float32) * (full_turn / IMG)
    cos_u = jnp.cos(turn_u)
    sin_u = jnp.sin(turn_u)
    real_part = samples[0] * samples[2]
    imag_part = samples[1] * samples[2]
    left = jnp.concatenate([real_part * cos_u - imag_part * sin_u, -(real_part * sin_u + imag_part * cos_u)], axis=1).astype(jnp.bfloat16)
    turn_v = jnp.mod(v_cells[:, None] * along_m[None, :], IMG).astype(jnp.float32) * (full_turn / IMG)
    right = jnp.concatenate([jnp.cos(turn_v), jnp.sin(turn_v)], axis=0).astype(jnp.bfloat16)
    return jnp.dot(left, right, preferred_element_type=jnp.float32)

def reference(visibilities, weights, uv_cells, flags, plan, beam, facets):
    inverse = jnp.argsort(plan).astype(jnp.int32)
    gains = beam[:, inverse]
    live = weights * flags.astype(jnp.float32)
    uv_float = uv_cells.astype(jnp.float32)

    def one_facet(record):
        position, gain_row = record

        def advance(running, entry):
            vis_block, live_block, uv_block, factor = entry
            samples = jnp.concatenate([vis_block, (live_block * factor)[None, :], uv_block], axis=0)
            return (running + facet_image(samples, position[0], position[1]), None)
        summed, _ = lax.scan(advance, jnp.zeros((P_SIZE, P_SIZE), jnp.float32), (visibilities, live, uv_float, gain_row))
        return summed
    images = lax.map(one_facet, (facets, gains))
    return images * (2.0 / math.sqrt(NBLK * KTOT))
```

```python
import functools
import math

import jax
import jax.numpy as jnp
from jax import lax
from jax.experimental import pallas as pl
from jax.experimental.pallas import tpu as pltpu
from jax.sharding import PartitionSpec as P

P_SIZE = 128
IMG = 32768
KEEP = 256
LANES = 128
HALF = P_SIZE // 2


def lane_prefix(flags):
    rows = lax.broadcasted_iota(jnp.int32, (LANES, LANES), 0)
    columns = lax.broadcasted_iota(jnp.int32, (LANES, LANES), 1)
    earlier = (rows < columns).astype(jnp.bfloat16)
    running = jnp.zeros((flags.shape[0], 1), jnp.float32)
    parts = []
    for start in range(0, flags.shape[1], LANES):
        piece = flags[:, start : start + LANES]
        inside = jnp.dot(piece.astype(jnp.bfloat16), earlier, preferred_element_type=jnp.float32)
        parts.append(inside + running)
        running = running + jnp.sum(piece, axis=1, keepdims=True)
    return jnp.concatenate(parts, axis=1)


def pack_kernel(copies, vis_ref, weight_ref, uv_ref, flag_ref, out_ref, data_ref):
    rows = weight_ref.shape[1]
    flags = flag_ref[...].astype(jnp.float32)
    weights = weight_ref[...]
    data_ref[0:2, :] = vis_ref[:, 0, :] * weights
    data_ref[2:4, :] = vis_ref[:, 1, :] * weights
    data_ref[4:6, :] = uv_ref[:, 0, :].astype(jnp.float32)
    data_ref[6:8, :] = uv_ref[:, 1, :].astype(jnp.float32)
    data = data_ref[...]
    high = data.astype(jnp.bfloat16).astype(jnp.float32)
    rest = data - high
    middle = rest.astype(jnp.bfloat16).astype(jnp.float32)
    low = rest - middle
    pieces = jnp.concatenate([high, middle, low], axis=0).astype(jnp.bfloat16)
    spot = jnp.where(flags > 0.0, lane_prefix(flags), -1.0).astype(jnp.int32)
    target = lax.broadcasted_iota(jnp.int32, (KEEP, rows), 0)
    packed = []
    for block in range(2):
        chosen = (target == spot[block : block + 1, :]).astype(jnp.float32).astype(jnp.bfloat16)
        moved = lax.dot_general(
            pieces, chosen, (((1,), (1,)), ((), ())), preferred_element_type=jnp.float32
        )
        packed.append(moved[0:8] + moved[8:16] + moved[16:24])
    parity = lax.broadcasted_iota(jnp.int32, packed[0].shape, 0) & 1
    result = jnp.where(parity == 0, packed[0], packed[1])
    for copy in range(copies):
        out_ref[copy, 0:8, :] = result[:, :LANES]
        out_ref[copy, 8:16, :] = result[:, LANES:]


def sine_cosine(turns):
    quarter = (turns + 8192) >> 14
    x = (turns - (quarter << 14)).astype(jnp.float32) * (2.0 * math.pi / 65536.0)
    y = x * x
    sine = x * (1.0 + y * (-1.0 / 6 + y * (1.0 / 120 + y * (-1.0 / 5040 + y * (1.0 / 362880)))))
    cosine = 1.0 + y * (-0.5 + y * (1.0 / 24 + y * (-1.0 / 720 + y * (1.0 / 40320))))
    odd = (quarter & 1) == 1
    first = jnp.where(odd, cosine, sine)
    second = jnp.where(odd, sine, cosine)
    first = jnp.where((quarter & 2) == 2, -first, first)
    second = jnp.where(((quarter + 1) & 2) == 2, -second, second)
    return first, second


def half_steps(turns, count):
    sine, cosine = sine_cosine(turns)
    twice = 4.0 * cosine * cosine - 2.0
    sines, cosines = [sine], [cosine]
    before_sine, before_cosine = -sine, cosine
    for _ in range(count - 1):
        sines.append(twice * sines[-1] - before_sine)
        cosines.append(twice * cosines[-1] - before_cosine)
        before_sine, before_cosine = sines[-2], cosines[-2]
    return sines, cosines


def unfold(values, reverse):
    shape = values.shape
    lane = lax.broadcasted_iota(jnp.int32, shape, 1)
    source = jnp.where((lane & 8) == 8, lane, lane ^ 7)
    values = jnp.take_along_axis(values, source, axis=1)
    if reverse:
        values = jnp.take_along_axis(values, 7 - lax.broadcasted_iota(jnp.int32, shape, 0), axis=0)
    return values


def image_kernel(
    scale, facet_ref, plan_ref, beam_ref, data_ref, keep_ref, send_ref,
    fine_v, fine_u, outer, coarse, order_ref,
):
    owners = data_ref.shape[0] // 16
    column = 2 * (facet_ref[0, 0] * P_SIZE - IMG // 2) + (P_SIZE - 1)
    row = 2 * (facet_ref[0, 1] * P_SIZE - IMG // 2) + (P_SIZE - 1)

    def advance(step, sums):
        first = pl.multiple_of((step >> 1) * 128, 128)
        member = step & 1
        owner = lax.broadcasted_iota(jnp.int32, (8, plan_ref.shape[1]), 0) + (step >> 1) * 8
        gain = jnp.sum(
            jnp.where(plan_ref[...] == 2 * owner + member, beam_ref[...], 0.0),
            axis=1,
            keepdims=True,
        )
        even, odd = sums
        for start in range(0, KEEP, LANES):
            real, imag, u, v = (
                data_ref[pl.ds(first + start // 16 + 2 * kind + member, 8, stride=16), :]
                for kind in range(4)
            )
            u = u.astype(jnp.int32)
            v = v.astype(jnp.int32)
            real = real * gain
            imag = imag * gain
            sine, cosine = sine_cosine(u * column + v * row)
            centre_real = real * cosine - imag * sine
            centre_imag = real * sine + imag * cosine
            sines, cosines = half_steps(v, 8)
            for tau in range(8):
                fine_v[0, pl.ds(tau, 8, stride=8), :] = cosines[tau]
                fine_v[1, pl.ds(tau, 8, stride=8), :] = sines[tau]
            sines, cosines = half_steps(u, 8)
            for tau in range(8):
                fine_u[0, pl.ds(tau, 8, stride=8), :] = cosines[tau]
                fine_u[1, pl.ds(tau, 8, stride=8), :] = sines[tau]
            sines, cosines = half_steps(u << 4, 4)
            for far in range(4):
                coarse[2 * far] = cosines[far]
                coarse[2 * far + 1] = sines[far]
            sines, cosines = half_steps(v << 4, 4)
            for far in range(4):
                rc, isn = centre_real * cosines[far], centre_imag * sines[far]
                ic, rs = centre_imag * cosines[far], centre_real * sines[far]
                above, below = 4 + far, 3 - far
                outer[2 * above] = rc - isn
                outer[2 * above + 1] = ic + rs
                outer[2 * below] = rc + isn
                outer[2 * below + 1] = ic - rs
            for pair in range(4):
                table_a, table_b, table_c, table_s = [], [], [], []
                for chunk in (2 * pair, 2 * pair + 1):
                    rows = pl.ds(8 * chunk, 8)
                    cos_f, sin_f = fine_v[0, rows, :], fine_v[1, rows, :]
                    part_a, part_b, part_c, part_s = [], [], [], []
                    for far in range(8):
                        x = jnp.broadcast_to(outer[2 * far, pl.ds(chunk, 1), :], (8, LANES))
                        y = jnp.broadcast_to(outer[2 * far + 1, pl.ds(chunk, 1), :], (8, LANES))
                        xc, ys, yc, xs = x * cos_f, y * sin_f, y * cos_f, x * sin_f
                        part_a += [xc + ys, xc - ys]
                        part_b += [yc - xs, yc + xs]
                    cos_f, sin_f = fine_u[0, rows, :], fine_u[1, rows, :]
                    for far in range(4):
                        x = jnp.broadcast_to(coarse[2 * far, pl.ds(chunk, 1), :], (8, LANES))
                        y = jnp.broadcast_to(coarse[2 * far + 1, pl.ds(chunk, 1), :], (8, LANES))
                        xc, ys, yc, xs = x * cos_f, y * sin_f, y * cos_f, x * sin_f
                        part_c += [xc + ys, xc - ys]
                        part_s += [yc - xs, yc + xs]
                    for table, part in (
                        (table_a, part_a), (table_b, part_b), (table_c, part_c), (table_s, part_s)
                    ):
                        table.append(jnp.concatenate(part, axis=0).astype(jnp.bfloat16))
                a, b, c, s = (
                    jnp.concatenate(table, axis=1) for table in (table_a, table_b, table_c, table_s)
                )
                contract = (((1,), (1,)), ((), ()))
                even = even + lax.dot_general(c, a, contract, preferred_element_type=jnp.float32)
                odd = odd + lax.dot_general(s, b, contract, preferred_element_type=jnp.float32)
        return even, odd

    zero = jnp.zeros((HALF, P_SIZE), jnp.float32)
    even, odd = lax.fori_loop(0, owners // 4, advance, (zero, zero))
    upper = (even - odd) * scale
    lower = (even + odd) * scale
    core = lax.axis_index("freq") & 1
    far = lax.axis_index("freq") >> 1
    for index in range(16):
        piece = index // 4
        slot = ((piece & 1) ^ core) * 2 + ((piece >> 1) ^ far)
        if index >= 8:
            source = index - 8
            values = unfold(upper[8 * source : 8 * source + 8], source % 2 == 0)
        else:
            source = 7 - index
            values = unfold(lower[8 * source : 8 * source + 8], source % 2 == 1)
        place = pl.multiple_of(slot * 32 + 8 * (index % 4), 8)
        order_ref[pl.ds(place, 8), :] = values
    keep_ref[...] = order_ref[0:HALF, :]
    send_ref[...] = order_ref[HALF:, :]


VMEM = pl.BlockSpec(memory_space=pltpu.VMEM)
SMEM = pl.BlockSpec(memory_space=pltpu.SMEM)


def body(total, facet_devices, visibilities, weights, uv_cells, flags, plan, beam, facets):
    packed = pl.pallas_call(
        functools.partial(pack_kernel, facet_devices),
        out_shape=jax.ShapeDtypeStruct((facet_devices, 16, LANES), jnp.float32),
        in_specs=[VMEM] * 4,
        out_specs=VMEM,
        scratch_shapes=[pltpu.VMEM((8, weights.shape[1]), jnp.float32)],
    )(visibilities, weights, uv_cells, flags)
    gathered = lax.all_to_all(packed, "facet", 0, 0)
    image = jax.ShapeDtypeStruct((HALF, P_SIZE), jnp.float32)
    keep, send = pl.pallas_call(
        functools.partial(image_kernel, 2.0 / math.sqrt(total)),
        out_shape=(image, image),
        in_specs=[SMEM, VMEM, VMEM, VMEM],
        out_specs=(VMEM, VMEM),
        scratch_shapes=[
            pltpu.VMEM((2, 64, LANES), jnp.float32),
            pltpu.VMEM((2, 64, LANES), jnp.float32),
            pltpu.VMEM((16, 8, LANES), jnp.float32),
            pltpu.VMEM((8, 8, LANES), jnp.float32),
            pltpu.VMEM((P_SIZE, P_SIZE), jnp.float32),
        ],
    )(facets, plan[None], beam, gathered.reshape(facet_devices * 16, LANES))
    half = keep + lax.ppermute(send, "freq", [(i, i ^ 1) for i in range(4)])
    return (half[:32] + lax.ppermute(half[32:], "freq", [(i, i ^ 2) for i in range(4)]))[None]


def solution(mesh):
    in_specs = (
        P("facet", None, "freq"),
        P("facet", "freq"),
        P("facet", None, "freq"),
        P("facet", "freq"),
        P(),
        P("facet", None),
        P("facet", None),
    )
    total = 64 * 2048
    return jax.shard_map(
        functools.partial(body, total, mesh.shape["facet"]),
        mesh=mesh,
        in_specs=in_specs,
        out_specs=P("facet", "freq", None),
        check_vma=False,
    )
```

```python
import functools
import math

import jax
import jax.numpy as jnp
from jax import lax
from jax.experimental import pallas as pl
from jax.experimental.pallas import tpu as pltpu
from jax.sharding import PartitionSpec as P

P_SIZE = 128
IMG = 32768
KEEP = 256
LANES = 128
HALF = P_SIZE // 2


def lane_prefix(flags):
    rows = lax.broadcasted_iota(jnp.int32, (LANES, LANES), 0)
    columns = lax.broadcasted_iota(jnp.int32, (LANES, LANES), 1)
    earlier = (rows < columns).astype(jnp.bfloat16)
    running = jnp.zeros((flags.shape[0], 1), jnp.float32)
    parts = []
    for start in range(0, flags.shape[1], LANES):
        piece = flags[:, start : start + LANES]
        inside = jnp.dot(piece.astype(jnp.bfloat16), earlier, preferred_element_type=jnp.float32)
        parts.append(inside + running)
        running = running + jnp.sum(piece, axis=1, keepdims=True)
    return jnp.concatenate(parts, axis=1)


def pack_kernel(copies, vis_ref, weight_ref, uv_ref, flag_ref, out_ref, data_ref):
    rows = weight_ref.shape[1]
    flags = flag_ref[...].astype(jnp.float32)
    weights = weight_ref[...]
    data_ref[0:2, :] = vis_ref[:, 0, :] * weights
    data_ref[2:4, :] = vis_ref[:, 1, :] * weights
    data_ref[4:6, :] = uv_ref[:, 0, :].astype(jnp.float32)
    data_ref[6:8, :] = uv_ref[:, 1, :].astype(jnp.float32)
    data = data_ref[...]
    high = data.astype(jnp.bfloat16).astype(jnp.float32)
    rest = data - high
    middle = rest.astype(jnp.bfloat16).astype(jnp.float32)
    low = rest - middle
    pieces = jnp.concatenate([high, middle, low], axis=0).astype(jnp.bfloat16)
    spot = jnp.where(flags > 0.0, lane_prefix(flags), -1.0).astype(jnp.int32)
    target = lax.broadcasted_iota(jnp.int32, (KEEP, rows), 0)
    packed = []
    for block in range(2):
        chosen = (target == spot[block : block + 1, :]).astype(jnp.float32).astype(jnp.bfloat16)
        moved = lax.dot_general(
            pieces, chosen, (((1,), (1,)), ((), ())), preferred_element_type=jnp.float32
        )
        packed.append(moved[0:8] + moved[8:16] + moved[16:24])
    parity = lax.broadcasted_iota(jnp.int32, packed[0].shape, 0) & 1
    result = jnp.where(parity == 0, packed[0], packed[1])
    for copy in range(copies):
        out_ref[copy, 0:8, :] = result[:, :LANES]
        out_ref[copy, 8:16, :] = result[:, LANES:]


def doubled(sine, cosine):
    twice = sine + sine
    return twice * cosine, 1.0 - twice * sine


def sine_cosine(turns):
    x = ((turns << 16) >> 16).astype(jnp.float32) * (2.0 * math.pi / 65536.0 / 4.0)
    y = x * x
    sine = x * (1.0 + y * (-1.0 / 6 + y * (1.0 / 120 + y * (-1.0 / 5040 + y * (1.0 / 362880)))))
    cosine = 1.0 + y * (-0.5 + y * (1.0 / 24 + y * (-1.0 / 720 + y * (1.0 / 40320))))
    return doubled(*doubled(sine, cosine))


def half_steps(sine, cosine, count):
    twice = 4.0 * cosine * cosine - 2.0
    sines, cosines = [sine], [cosine]
    before_sine, before_cosine = -sine, cosine
    for _ in range(count - 1):
        sines.append(twice * sines[-1] - before_sine)
        cosines.append(twice * cosines[-1] - before_cosine)
        before_sine, before_cosine = sines[-2], cosines[-2]
    return sines, cosines


def chunk_tables(outer, fine, count, chunk):
    cosine, sine = fine[0, pl.ds(8 * chunk, 8), :], fine[1, pl.ds(8 * chunk, 8), :]
    first, second = [], []
    for far in range(count):
        x = jnp.broadcast_to(outer[2 * far, pl.ds(chunk, 1), :], (8, LANES))
        y = jnp.broadcast_to(outer[2 * far + 1, pl.ds(chunk, 1), :], (8, LANES))
        first += [x * cosine, y * sine]
        second += [y * cosine, x * sine]
    return (
        jnp.concatenate(first, axis=0).astype(jnp.bfloat16),
        jnp.concatenate(second, axis=0).astype(jnp.bfloat16),
    )


def prepare(centre, data_ref, gain_ref, step, half, buffers):
    fine_v, fine_u, outer, coarse = buffers
    column, row = centre
    tile = step >> 1
    member = step & 1
    gain = gain_ref[pl.ds(pl.multiple_of(member * (gain_ref.shape[0] // 2) + tile * 8, 8), 8), :]
    first = tile * 128 + 8 * half + member
    real, imag, u, v = (
        data_ref[pl.ds(first + 2 * kind, 8, stride=16), :] for kind in range(4)
    )
    u = u.astype(jnp.int32)
    v = v.astype(jnp.int32)
    real = real * gain
    imag = imag * gain
    sine, cosine = sine_cosine(u * column + v * row)
    centre_real = real * cosine - imag * sine
    centre_imag = real * sine + imag * cosine
    near_v = sine_cosine(v)
    near_u = sine_cosine(u)
    for near, fine in ((near_v, fine_v), (near_u, fine_u)):
        sines, cosines = half_steps(*near, 8)
        for tau in range(8):
            fine[0, pl.ds(tau, 8, stride=8), :] = cosines[tau]
            fine[1, pl.ds(tau, 8, stride=8), :] = sines[tau]
    for _ in range(4):
        near_v = doubled(*near_v)
        near_u = doubled(*near_u)
    sines, cosines = half_steps(*near_u, 4)
    for far in range(4):
        coarse[2 * far] = cosines[far]
        coarse[2 * far + 1] = sines[far]
    sines, cosines = half_steps(*near_v, 4)
    for far in range(4):
        rc, isn = centre_real * cosines[far], centre_imag * sines[far]
        ic, rs = centre_imag * cosines[far], centre_real * sines[far]
        above, below = 4 + far, 3 - far
        outer[2 * above] = rc - isn
        outer[2 * above + 1] = ic + rs
        outer[2 * below] = rc + isn
        outer[2 * below + 1] = ic - rs


def accumulate(buffers, sums):
    fine_v, fine_u, outer, coarse = buffers
    even, odd = sums
    for pair in range(4):
        tables = [
            chunk_tables(coarse, fine_u, 4, chunk) + chunk_tables(outer, fine_v, 8, chunk)
            for chunk in (2 * pair, 2 * pair + 1)
        ]
        c, s, a, b = (jnp.concatenate(table, axis=1) for table in zip(*tables))
        contract = (((1,), (1,)), ((), ()))
        even = even + lax.dot_general(c, a, contract, preferred_element_type=jnp.float32)
        odd = odd + lax.dot_general(s, b, contract, preferred_element_type=jnp.float32)
    return even, odd


def paired(values, source, reverse):
    values = jnp.take_along_axis(values, source, axis=1)
    if reverse:
        values = jnp.take_along_axis(
            values, 7 - lax.broadcasted_iota(jnp.int32, values.shape, 0), axis=0
        )
    return values


def sum_blocks(block_of, facet_ref, plan_ref, beam_ref, data_ref, scratch, sums):
    gain_ref, buffers = scratch[0], (scratch[1:5], scratch[5:9])
    owners = data_ref.shape[0] // 16
    centre = tuple(2 * (facet_ref[0, k] * P_SIZE - IMG // 2) + (P_SIZE - 1) for k in range(2))
    for member in range(2):
        owner = lax.broadcasted_iota(jnp.int32, (owners, plan_ref.shape[1]), 0)
        matches = plan_ref[...] == block_of(owner, member)
        gain = jnp.sum(jnp.where(matches, beam_ref[...], 0.0), axis=1, keepdims=True)
        gain_ref[member * owners : (member + 1) * owners, :] = jnp.broadcast_to(
            gain, (owners, LANES)
        )
    steps = owners // 4
    prepare(centre, data_ref, gain_ref, 0, 0, buffers[0])

    def advance(step, sums):
        prepare(centre, data_ref, gain_ref, step, 1, buffers[1])
        sums = accumulate(buffers[0], sums)
        prepare(centre, data_ref, gain_ref, (step + 1) & (steps - 1), 0, buffers[0])
        return accumulate(buffers[1], sums)

    return lax.fori_loop(0, steps, advance, sums)


def first_kernel(facet_ref, plan_ref, beam_ref, data_ref, even_ref, odd_ref, *scratch):
    side = lax.axis_index("facet") & 1
    zero = jnp.zeros((HALF, P_SIZE), jnp.float32)
    even, odd = sum_blocks(
        lambda owner, member: 4 * owner + 2 * side + member,
        facet_ref, plan_ref, beam_ref, data_ref, scratch, (zero, zero),
    )
    even_ref[...] = even
    odd_ref[...] = odd


def last_kernel(
    scale, facet_ref, plan_ref, beam_ref, data_ref, even_ref, odd_ref, keep_ref, send_ref,
    order_ref, *scratch,
):
    side = 1 - (lax.axis_index("facet") & 1)
    even, odd = sum_blocks(
        lambda owner, member: 4 * owner + 2 * side + member,
        facet_ref, plan_ref, beam_ref, data_ref, scratch, (even_ref[...], odd_ref[...]),
    )
    even, odd = even * scale, odd * scale
    core = lax.axis_index("freq") & 1
    far = lax.axis_index("freq") >> 1
    lane = lax.broadcasted_iota(jnp.int32, (8, P_SIZE), 1)
    near = jnp.where((lane & 8) == 8, lane ^ 8, lane ^ 7)
    sign = jnp.where((lane & 8) == 8, -1.0, 1.0)
    for block in range(8):
        base = 16 * (block // 2)
        above = block % 2 == 1
        even_p, even_q = even[base : base + 8], even[base + 8 : base + 16]
        odd_p, odd_q = odd[base : base + 8], odd[base + 8 : base + 16]
        even_row = even_p - even_q if above else even_p + even_q
        odd_row = odd_p + odd_q if above else odd_p - odd_q
        less, more = even_row - odd_row, even_row + odd_row
        for index, one, two, reverse in (
            (8 + block, less, more, not above),
            (7 - block, more, less, above),
        ):
            values = paired(one, near, reverse) + sign * paired(two, near ^ 8, reverse)
            piece = index // 4
            slot = ((piece & 1) ^ core) * 2 + ((piece >> 1) ^ far)
            place = pl.multiple_of(slot * 32 + 8 * (index % 4), 8)
            order_ref[pl.ds(place, 8), :] = values
    keep_ref[...] = order_ref[0:HALF, :]
    send_ref[...] = order_ref[HALF:, :]


SMALL = pltpu.CompilerParams(vmem_limit_bytes=8 << 20)
VMEM = pl.BlockSpec(memory_space=pltpu.VMEM)
SMEM = pl.BlockSpec(memory_space=pltpu.SMEM)


def body(total, plane, visibilities, weights, uv_cells, flags, plan, beam, facets):
    packed = pl.pallas_call(
        functools.partial(pack_kernel, plane),
        out_shape=jax.ShapeDtypeStruct((plane, 16, LANES), jnp.float32),
        in_specs=[VMEM] * 4,
        out_specs=VMEM,
        scratch_shapes=[pltpu.VMEM((8, weights.shape[1]), jnp.float32)],
        compiler_params=SMALL,
    )(visibilities, weights, uv_cells, flags)
    groups = [list(range(side, 2 * plane, 2)) for side in range(2)]
    near = lax.all_to_all(packed, "facet", 0, 0, axis_index_groups=groups)
    near = near.reshape(plane * 16, LANES)
    far = lax.ppermute(near, "facet", [(i, i ^ 1) for i in range(2 * plane)])
    image = jax.ShapeDtypeStruct((HALF, P_SIZE), jnp.float32)
    buffers = [
        pltpu.VMEM((2, 64, LANES), jnp.float32),
        pltpu.VMEM((2, 64, LANES), jnp.float32),
        pltpu.VMEM((16, 8, LANES), jnp.float32),
        pltpu.VMEM((8, 8, LANES), jnp.float32),
    ]
    scratch = [pltpu.VMEM((2 * plane, LANES), jnp.float32)] + buffers * 2
    cost = pl.CostEstimate(
        flops=2 * 2 * HALF * P_SIZE * 2 * plane * KEEP, bytes_accessed=1 << 18, transcendentals=0
    )
    even, odd = pl.pallas_call(
        first_kernel,
        out_shape=(image, image),
        in_specs=[SMEM, VMEM, VMEM, VMEM],
        out_specs=(VMEM, VMEM),
        scratch_shapes=scratch,
        compiler_params=SMALL,
        cost_estimate=cost,
    )(facets, plan[None], beam, near)
    keep, send = pl.pallas_call(
        functools.partial(last_kernel, 2.0 / math.sqrt(total)),
        out_shape=(image, image),
        in_specs=[SMEM, VMEM, VMEM, VMEM, VMEM, VMEM],
        out_specs=(VMEM, VMEM),
        scratch_shapes=[pltpu.VMEM((P_SIZE, P_SIZE), jnp.float32)] + scratch,
        compiler_params=SMALL,
        cost_estimate=cost,
    )(facets, plan[None], beam, far, even, odd)
    half = keep + lax.ppermute(send, "freq", [(i, i ^ 1) for i in range(4)])
    return (half[:32] + lax.ppermute(half[32:], "freq", [(i, i ^ 2) for i in range(4)]))[None]


def solution(mesh):
    in_specs = (
        P("facet", None, "freq"),
        P("facet", "freq"),
        P("facet", None, "freq"),
        P("facet", "freq"),
        P(),
        P("facet", None),
        P("facet", None),
    )
    total = 64 * 2048
    return jax.shard_map(
        functools.partial(body, total, mesh.shape["facet"] // 2),
        mesh=mesh,
        in_specs=in_specs,
        out_specs=P("facet", "freq", None),
        check_vma=False,
    )
```

```python
import functools
import math

import jax
import jax.numpy as jnp
from jax import lax
from jax.experimental import pallas as pl
from jax.experimental.pallas import tpu as pltpu
from jax.sharding import PartitionSpec as P

P_SIZE = 128
IMG = 32768
KEEP = 256
LANES = 128
HALF = P_SIZE // 2


def lane_prefix(flags):
    rows = lax.broadcasted_iota(jnp.int32, (LANES, LANES), 0)
    columns = lax.broadcasted_iota(jnp.int32, (LANES, LANES), 1)
    earlier = (rows < columns).astype(jnp.bfloat16)
    running = jnp.zeros((flags.shape[0], 1), jnp.float32)
    parts = []
    for start in range(0, flags.shape[1], LANES):
        piece = flags[:, start : start + LANES]
        inside = jnp.dot(piece.astype(jnp.bfloat16), earlier, preferred_element_type=jnp.float32)
        parts.append(inside + running)
        running = running + jnp.sum(piece, axis=1, keepdims=True)
    return jnp.concatenate(parts, axis=1)


def pack_kernel(
    vis_in, weight_in, uv_in, flag_in, plan_in, beam_in, facet_in,
    out_ref, gain_ref, centre_ref,
    vis_ref, weight_ref, uv_ref, flag_ref, plan_ref, beam_ref, facet_ref, data_ref, arrived,
):
    copies = [
        pltpu.make_async_copy(source, target, arrived.at[index])
        for index, (source, target) in enumerate(
            (
                (flag_in, flag_ref), (vis_in, vis_ref), (weight_in, weight_ref), (uv_in, uv_ref),
                (plan_in, plan_ref), (beam_in, beam_ref), (facet_in, facet_ref),
            )
        )
    ]
    for copy in copies:
        copy.start()
    for copy in copies:
        copy.wait()
    rows = weight_ref.shape[1]
    flags = flag_ref[...].astype(jnp.float32)
    weights = weight_ref[...]
    data_ref[0:2, :] = vis_ref[:, 0, :] * weights
    data_ref[2:4, :] = vis_ref[:, 1, :] * weights
    data_ref[4:6, :] = uv_ref[:, 0, :].astype(jnp.float32)
    data_ref[6:8, :] = uv_ref[:, 1, :].astype(jnp.float32)
    data = data_ref[...]
    high = data.astype(jnp.bfloat16).astype(jnp.float32)
    rest = data - high
    middle = rest.astype(jnp.bfloat16).astype(jnp.float32)
    low = rest - middle
    pieces = jnp.concatenate([high, middle, low], axis=0).astype(jnp.bfloat16)
    spot = jnp.where(flags > 0.0, lane_prefix(flags), -1.0).astype(jnp.int32)
    target = lax.broadcasted_iota(jnp.int32, (KEEP, rows), 0)
    packed = []
    for block in range(2):
        chosen = (target == spot[block : block + 1, :]).astype(jnp.float32).astype(jnp.bfloat16)
        moved = lax.dot_general(
            pieces, chosen, (((1,), (1,)), ((), ())), preferred_element_type=jnp.float32
        )
        packed.append(moved[0:8] + moved[8:16] + moved[16:24])
    parity = lax.broadcasted_iota(jnp.int32, packed[0].shape, 0) & 1
    result = jnp.where(parity == 0, packed[0], packed[1])
    plane = out_ref.shape[0]
    for peer in range(plane):
        out_ref[peer, 0:8, :] = result[:, :LANES]
        out_ref[peer, 8:16, :] = result[:, LANES:]
    side = lax.axis_index("facet") & 1
    shape = (plane, plan_ref.shape[1])
    for which in range(2):
        for member in range(2):
            block = 4 * lax.broadcasted_iota(jnp.int32, shape, 0) + 2 * (side ^ which) + member
            matches = plan_ref[...] == block
            gain = jnp.sum(jnp.where(matches, beam_ref[...], 0.0), axis=1, keepdims=True)
            first = (2 * which + member) * plane
            gain_ref[first : first + plane, :] = jnp.broadcast_to(gain, (plane, LANES))
    for axis in range(2):
        centre = 2 * (facet_ref[0:1, axis : axis + 1] * P_SIZE - IMG // 2) + (P_SIZE - 1)
        centre_ref[8 * axis : 8 * axis + 8, :] = jnp.broadcast_to(centre, (8, LANES))


def doubled(sine, cosine):
    twice = sine + sine
    return twice * cosine, 1.0 - twice * sine


def sine_cosine(turns):
    x = ((turns << 16) >> 16).astype(jnp.float32) * (2.0 * math.pi / 65536.0 / 4.0)
    y = x * x
    sine = x * (1.0 + y * (-1.0 / 6 + y * (1.0 / 120 + y * (-1.0 / 5040 + y * (1.0 / 362880)))))
    cosine = 1.0 + y * (-0.5 + y * (1.0 / 24 + y * (-1.0 / 720 + y * (1.0 / 40320))))
    return doubled(*doubled(sine, cosine))


def half_steps(sine, cosine, count):
    twice = 4.0 * cosine * cosine - 2.0
    sines, cosines = [sine], [cosine]
    before_sine, before_cosine = -sine, cosine
    for _ in range(count - 1):
        sines.append(twice * sines[-1] - before_sine)
        cosines.append(twice * cosines[-1] - before_cosine)
        before_sine, before_cosine = sines[-2], cosines[-2]
    return sines, cosines


def chunk_tables(outer, fine, count, chunk):
    cosine, sine = fine[0, pl.ds(8 * chunk, 8), :], fine[1, pl.ds(8 * chunk, 8), :]
    first, second = [], []
    for far in range(count):
        x = jnp.broadcast_to(outer[2 * far, pl.ds(chunk, 1), :], (8, LANES))
        y = jnp.broadcast_to(outer[2 * far + 1, pl.ds(chunk, 1), :], (8, LANES))
        first += [x * cosine, y * sine]
        second += [y * cosine, x * sine]
    return (
        jnp.concatenate(first, axis=0).astype(jnp.bfloat16),
        jnp.concatenate(second, axis=0).astype(jnp.bfloat16),
    )


def prepare(which, centre_ref, data_ref, gain_ref, step, half, buffers):
    fine_v, fine_u, outer, coarse = buffers
    column, row = centre_ref[0:8, :], centre_ref[8:16, :]
    tile = step >> 1
    member = step & 1
    owners = gain_ref.shape[0] // 4
    gain = gain_ref[pl.ds(pl.multiple_of((2 * which + member) * owners + tile * 8, 8), 8), :]
    first = tile * 128 + 8 * half + member
    real, imag, u, v = (
        data_ref[pl.ds(first + 2 * kind, 8, stride=16), :] for kind in range(4)
    )
    u = u.astype(jnp.int32)
    v = v.astype(jnp.int32)
    real = real * gain
    imag = imag * gain
    sine, cosine = sine_cosine(u * column + v * row)
    centre_real = real * cosine - imag * sine
    centre_imag = real * sine + imag * cosine
    near_v = sine_cosine(v)
    near_u = sine_cosine(u)
    for near, fine in ((near_v, fine_v), (near_u, fine_u)):
        sines, cosines = half_steps(*near, 8)
        for tau in range(8):
            fine[0, pl.ds(tau, 8, stride=8), :] = cosines[tau]
            fine[1, pl.ds(tau, 8, stride=8), :] = sines[tau]
    for _ in range(4):
        near_v = doubled(*near_v)
        near_u = doubled(*near_u)
    sines, cosines = half_steps(*near_u, 4)
    for far in range(4):
        coarse[2 * far] = cosines[far]
        coarse[2 * far + 1] = sines[far]
    sines, cosines = half_steps(*near_v, 4)
    for far in range(4):
        rc, isn = centre_real * cosines[far], centre_imag * sines[far]
        ic, rs = centre_imag * cosines[far], centre_real * sines[far]
        above, below = 4 + far, 3 - far
        outer[2 * above] = rc - isn
        outer[2 * above + 1] = ic + rs
        outer[2 * below] = rc + isn
        outer[2 * below + 1] = ic - rs


def accumulate(buffers, sums):
    fine_v, fine_u, outer, coarse = buffers
    even, odd = sums
    for pair in range(4):
        tables = [
            chunk_tables(coarse, fine_u, 4, chunk) + chunk_tables(outer, fine_v, 8, chunk)
            for chunk in (2 * pair, 2 * pair + 1)
        ]
        c, s, a, b = (jnp.concatenate(table, axis=1) for table in zip(*tables))
        contract = (((1,), (1,)), ((), ()))
        even = even + lax.dot_general(c, a, contract, preferred_element_type=jnp.float32)
        odd = odd + lax.dot_general(s, b, contract, preferred_element_type=jnp.float32)
    return even, odd


def paired(values, source, reverse):
    values = jnp.take_along_axis(values, source, axis=1)
    if reverse:
        values = jnp.take_along_axis(
            values, 7 - lax.broadcasted_iota(jnp.int32, values.shape, 0), axis=0
        )
    return values


def sum_blocks(which, centre_ref, gain_ref, data_ref, scratch, sums):
    buffers = (scratch[0:4], scratch[4:8])
    source = (which, centre_ref, data_ref, gain_ref)
    steps = data_ref.shape[0] // 64
    prepare(*source, 0, 0, buffers[0])

    def advance(step, sums):
        prepare(*source, step, 1, buffers[1])
        sums = accumulate(buffers[0], sums)
        prepare(*source, (step + 1) & (steps - 1), 0, buffers[0])
        return accumulate(buffers[1], sums)

    return lax.fori_loop(0, steps, advance, sums)


def first_kernel(centre_ref, gain_ref, data_ref, even_ref, odd_ref, *scratch):
    zero = jnp.zeros((HALF, P_SIZE), jnp.float32)
    even, odd = sum_blocks(0, centre_ref, gain_ref, data_ref, scratch, (zero, zero))
    even_ref[...] = even
    odd_ref[...] = odd


def last_kernel(
    scale, centre_ref, gain_ref, data_ref, even_ref, odd_ref, keep_ref, send_ref,
    order_ref, *scratch,
):
    even, odd = sum_blocks(
        1, centre_ref, gain_ref, data_ref, scratch, (even_ref[...], odd_ref[...])
    )
    even, odd = even * scale, odd * scale
    core = lax.axis_index("freq") & 1
    far = lax.axis_index("freq") >> 1
    lane = lax.broadcasted_iota(jnp.int32, (8, P_SIZE), 1)
    near = jnp.where((lane & 8) == 8, lane ^ 8, lane ^ 7)
    sign = jnp.where((lane & 8) == 8, -1.0, 1.0)
    for block in range(8):
        base = 16 * (block // 2)
        above = block % 2 == 1
        even_p, even_q = even[base : base + 8], even[base + 8 : base + 16]
        odd_p, odd_q = odd[base : base + 8], odd[base + 8 : base + 16]
        even_row = even_p - even_q if above else even_p + even_q
        odd_row = odd_p + odd_q if above else odd_p - odd_q
        less, more = even_row - odd_row, even_row + odd_row
        for index, one, two, reverse in (
            (8 + block, less, more, not above),
            (7 - block, more, less, above),
        ):
            values = paired(one, near, reverse) + sign * paired(two, near ^ 8, reverse)
            piece = index // 4
            slot = ((piece & 1) ^ core) * 2 + ((piece >> 1) ^ far)
            place = pl.multiple_of(slot * 32 + 8 * (index % 4), 8)
            order_ref[pl.ds(place, 8), :] = values
    keep_ref[...] = order_ref[0:HALF, :]
    send_ref[...] = order_ref[HALF:, :]


SMALL = pltpu.CompilerParams(vmem_limit_bytes=8 << 20)
VMEM = pl.BlockSpec(memory_space=pltpu.VMEM)


def body(total, plane, visibilities, weights, uv_cells, flags, plan, beam, facets):
    arguments = (visibilities, weights, uv_cells, flags, plan[None], beam, facets)
    packed, gains, centre = pl.pallas_call(
        pack_kernel,
        out_shape=(
            jax.ShapeDtypeStruct((plane, 16, LANES), jnp.float32),
            jax.ShapeDtypeStruct((4 * plane, LANES), jnp.float32),
            jax.ShapeDtypeStruct((16, LANES), jnp.int32),
        ),
        in_specs=[pl.BlockSpec(memory_space=pltpu.HBM)] * 7,
        out_specs=(VMEM, VMEM, VMEM),
        scratch_shapes=[pltpu.VMEM(each.shape, each.dtype) for each in arguments]
        + [
            pltpu.VMEM((8, weights.shape[1]), jnp.float32),
            pltpu.SemaphoreType.DMA((len(arguments),)),
        ],
        compiler_params=SMALL,
    )(*(pltpu.with_memory_space_constraint(each, pltpu.HBM) for each in arguments))
    groups = [list(range(side, 2 * plane, 2)) for side in range(2)]
    near = lax.all_to_all(packed, "facet", 0, 0, axis_index_groups=groups)
    near = near.reshape(plane * 16, LANES)
    far = lax.ppermute(near, "facet", [(i, i ^ 1) for i in range(2 * plane)])
    image = jax.ShapeDtypeStruct((HALF, P_SIZE), jnp.float32)
    buffers = [
        pltpu.VMEM((2, 64, LANES), jnp.float32),
        pltpu.VMEM((2, 64, LANES), jnp.float32),
        pltpu.VMEM((16, 8, LANES), jnp.float32),
        pltpu.VMEM((8, 8, LANES), jnp.float32),
    ]
    scratch = buffers * 2
    cost = pl.CostEstimate(
        flops=2 * 2 * HALF * P_SIZE * 2 * plane * KEEP, bytes_accessed=1 << 18, transcendentals=0
    )
    even, odd = pl.pallas_call(
        first_kernel,
        out_shape=(image, image),
        in_specs=[VMEM] * 3,
        out_specs=(VMEM, VMEM),
        scratch_shapes=scratch,
        compiler_params=SMALL,
        cost_estimate=cost,
    )(centre, gains, near)
    keep, send = pl.pallas_call(
        functools.partial(last_kernel, 2.0 / math.sqrt(total)),
        out_shape=(image, image),
        in_specs=[VMEM] * 5,
        out_specs=(VMEM, VMEM),
        scratch_shapes=[pltpu.VMEM((P_SIZE, P_SIZE), jnp.float32)] + scratch,
        compiler_params=SMALL,
        cost_estimate=cost,
    )(centre, gains, far, even, odd)
    half = keep + lax.ppermute(send, "freq", [(i, i ^ 1) for i in range(4)])
    return (half[:32] + lax.ppermute(half[32:], "freq", [(i, i ^ 2) for i in range(4)]))[None]


def solution(mesh):
    in_specs = (
        P("facet", None, "freq"),
        P("facet", "freq"),
        P("facet", None, "freq"),
        P("facet", "freq"),
        P(),
        P("facet", None),
        P("facet", None),
    )
    total = 64 * 2048
    return jax.shard_map(
        functools.partial(body, total, mesh.shape["facet"] // 2),
        mesh=mesh,
        in_specs=in_specs,
        out_specs=P("facet", "freq", None),
        check_vma=False,
    )
```

```python
import functools
import math

import jax
import jax.numpy as jnp
from jax import lax
from jax.experimental import pallas as pl
from jax.experimental.pallas import tpu as pltpu
from jax.sharding import PartitionSpec as P

P_SIZE = 128
IMG = 32768
KEEP = 256
LANES = 128
HALF = P_SIZE // 2


def lane_prefix(flags):
    rows = lax.broadcasted_iota(jnp.int32, (LANES, LANES), 0)
    columns = lax.broadcasted_iota(jnp.int32, (LANES, LANES), 1)
    earlier = (rows < columns).astype(jnp.bfloat16)
    running = jnp.zeros((flags.shape[0], 1), jnp.float32)
    parts = []
    for start in range(0, flags.shape[1], LANES):
        piece = flags[:, start : start + LANES]
        inside = jnp.dot(piece.astype(jnp.bfloat16), earlier, preferred_element_type=jnp.float32)
        parts.append(inside + running)
        running = running + jnp.sum(piece, axis=1, keepdims=True)
    return jnp.concatenate(parts, axis=1)


def pack_kernel(
    vis_in, weight_in, uv_in, flag_in, plan_in, beam_in, facet_in,
    out_ref, mine_ref, other_ref,
    vis_ref, weight_ref, uv_ref, flag_ref, plan_ref, beam_ref, facet_ref, data_ref, arrived,
):
    copies = [
        pltpu.make_async_copy(source, target, arrived.at[index])
        for index, (source, target) in enumerate(
            (
                (flag_in, flag_ref), (vis_in, vis_ref), (weight_in, weight_ref), (uv_in, uv_ref),
                (plan_in, plan_ref), (beam_in, beam_ref), (facet_in, facet_ref),
            )
        )
    ]
    for copy in copies:
        copy.start()
    for copy in copies:
        copy.wait()
    rows = weight_ref.shape[1]
    flags = flag_ref[...].astype(jnp.float32)
    weights = weight_ref[...]
    data_ref[0:2, :] = vis_ref[:, 0, :] * weights
    data_ref[2:4, :] = vis_ref[:, 1, :] * weights
    data_ref[4:6, :] = uv_ref[:, 0, :].astype(jnp.float32)
    data_ref[6:8, :] = uv_ref[:, 1, :].astype(jnp.float32)
    data = data_ref[...]
    high = data.astype(jnp.bfloat16).astype(jnp.float32)
    rest = data - high
    middle = rest.astype(jnp.bfloat16).astype(jnp.float32)
    low = rest - middle
    pieces = jnp.concatenate([high, middle, low], axis=0).astype(jnp.bfloat16)
    spot = jnp.where(flags > 0.0, lane_prefix(flags), -1.0).astype(jnp.int32)
    target = lax.broadcasted_iota(jnp.int32, (KEEP, rows), 0)
    packed = []
    for block in range(2):
        chosen = (target == spot[block : block + 1, :]).astype(jnp.float32).astype(jnp.bfloat16)
        moved = lax.dot_general(
            pieces, chosen, (((1,), (1,)), ((), ())), preferred_element_type=jnp.float32
        )
        packed.append(moved[0:8] + moved[8:16] + moved[16:24])
    parity = lax.broadcasted_iota(jnp.int32, packed[0].shape, 0) & 1
    result = jnp.where(parity == 0, packed[0], packed[1])
    plane = out_ref.shape[0]
    for peer in range(plane):
        out_ref[peer, 0:8, :] = result[:, :LANES]
        out_ref[peer, 8:16, :] = result[:, LANES:]
    side = lax.axis_index("facet") & 1
    shape = (plane, plan_ref.shape[1])
    for which, note_ref in ((0, mine_ref), (1, other_ref)):
        for axis in range(2):
            centre = 2 * (facet_ref[0:1, axis : axis + 1] * P_SIZE - IMG // 2) + (P_SIZE - 1)
            note_ref[8 * axis : 8 * axis + 8, :] = jnp.broadcast_to(
                centre.astype(jnp.float32), (8, LANES)
            )
        for member in range(2):
            block = 4 * lax.broadcasted_iota(jnp.int32, shape, 0) + 2 * (side ^ which) + member
            matches = plan_ref[...] == block
            gain = jnp.sum(jnp.where(matches, beam_ref[...], 0.0), axis=1, keepdims=True)
            first = 16 + member * plane
            note_ref[first : first + plane, :] = jnp.broadcast_to(gain, (plane, LANES))


def doubled(sine, cosine):
    twice = sine + sine
    return twice * cosine, 1.0 - twice * sine


def sine_cosine(turns):
    x = ((turns << 16) >> 16).astype(jnp.float32) * (2.0 * math.pi / 65536.0 / 4.0)
    y = x * x
    sine = x * (1.0 + y * (-1.0 / 6 + y * (1.0 / 120 + y * (-1.0 / 5040 + y * (1.0 / 362880)))))
    cosine = 1.0 + y * (-0.5 + y * (1.0 / 24 + y * (-1.0 / 720 + y * (1.0 / 40320))))
    return doubled(*doubled(sine, cosine))


def half_steps(sine, cosine, count):
    twice = 4.0 * cosine * cosine - 2.0
    sines, cosines = [sine], [cosine]
    before_sine, before_cosine = -sine, cosine
    for _ in range(count - 1):
        sines.append(twice * sines[-1] - before_sine)
        cosines.append(twice * cosines[-1] - before_cosine)
        before_sine, before_cosine = sines[-2], cosines[-2]
    return sines, cosines


def chunk_tables(outer, fine, count, chunk):
    cosine, sine = fine[0, pl.ds(8 * chunk, 8), :], fine[1, pl.ds(8 * chunk, 8), :]
    first, second = [], []
    for far in range(count):
        x = jnp.broadcast_to(outer[2 * far, pl.ds(chunk, 1), :], (8, LANES))
        y = jnp.broadcast_to(outer[2 * far + 1, pl.ds(chunk, 1), :], (8, LANES))
        first += [x * cosine, y * sine]
        second += [y * cosine, x * sine]
    return (
        jnp.concatenate(first, axis=0).astype(jnp.bfloat16),
        jnp.concatenate(second, axis=0).astype(jnp.bfloat16),
    )


def prepare(note_ref, data_ref, step, half, buffers):
    fine_v, fine_u, outer, coarse = buffers
    column = note_ref[0:8, :].astype(jnp.int32)
    row = note_ref[8:16, :].astype(jnp.int32)
    tile = step >> 1
    member = step & 1
    place = 16 + member * (data_ref.shape[0] // 16) + tile * 8
    gain = note_ref[pl.ds(pl.multiple_of(place, 8), 8), :]
    first = tile * 128 + 8 * half + member
    real, imag, u, v = (
        data_ref[pl.ds(first + 2 * kind, 8, stride=16), :] for kind in range(4)
    )
    u = u.astype(jnp.int32)
    v = v.astype(jnp.int32)
    real = real * gain
    imag = imag * gain
    sine, cosine = sine_cosine(u * column + v * row)
    centre_real = real * cosine - imag * sine
    centre_imag = real * sine + imag * cosine
    near_v = sine_cosine(v)
    near_u = sine_cosine(u)
    for near, fine in ((near_v, fine_v), (near_u, fine_u)):
        sines, cosines = half_steps(*near, 8)
        for tau in range(8):
            fine[0, pl.ds(tau, 8, stride=8), :] = cosines[tau]
            fine[1, pl.ds(tau, 8, stride=8), :] = sines[tau]
    for _ in range(4):
        near_v = doubled(*near_v)
        near_u = doubled(*near_u)
    sines, cosines = half_steps(*near_u, 4)
    for far in range(4):
        coarse[2 * far] = cosines[far]
        coarse[2 * far + 1] = sines[far]
    sines, cosines = half_steps(*near_v, 4)
    for far in range(4):
        rc, isn = centre_real * cosines[far], centre_imag * sines[far]
        ic, rs = centre_imag * cosines[far], centre_real * sines[far]
        above, below = 4 + far, 3 - far
        outer[2 * above] = rc - isn
        outer[2 * above + 1] = ic + rs
        outer[2 * below] = rc + isn
        outer[2 * below + 1] = ic - rs


def accumulate(buffers, sums):
    fine_v, fine_u, outer, coarse = buffers
    even, odd = sums
    for pair in range(4):
        tables = [
            chunk_tables(coarse, fine_u, 4, chunk) + chunk_tables(outer, fine_v, 8, chunk)
            for chunk in (2 * pair, 2 * pair + 1)
        ]
        c, s, a, b = (jnp.concatenate(table, axis=1) for table in zip(*tables))
        contract = (((1,), (1,)), ((), ()))
        even = even + lax.dot_general(c, a, contract, preferred_element_type=jnp.float32)
        odd = odd + lax.dot_general(s, b, contract, preferred_element_type=jnp.float32)
    return even, odd


def paired(values, source, reverse):
    values = jnp.take_along_axis(values, source, axis=1)
    if reverse:
        values = jnp.take_along_axis(
            values, 7 - lax.broadcasted_iota(jnp.int32, values.shape, 0), axis=0
        )
    return values


def image_kernel(scale, swap, note_ref, data_ref, image_ref, *scratch):
    buffers = (scratch[0:4], scratch[4:8])
    steps = data_ref.shape[0] // 64
    prepare(note_ref, data_ref, 0, 0, buffers[0])

    def advance(step, sums):
        prepare(note_ref, data_ref, step, 1, buffers[1])
        sums = accumulate(buffers[0], sums)
        prepare(note_ref, data_ref, (step + 1) & (steps - 1), 0, buffers[0])
        return accumulate(buffers[1], sums)

    zero = jnp.zeros((HALF, P_SIZE), jnp.float32)
    even, odd = lax.fori_loop(0, steps, advance, (zero, zero))
    even, odd = even * scale, odd * scale
    core = lax.axis_index("freq") & 1
    far = (lax.axis_index("freq") >> 1) ^ swap
    lane = lax.broadcasted_iota(jnp.int32, (8, P_SIZE), 1)
    near = jnp.where((lane & 8) == 8, lane ^ 8, lane ^ 7)
    sign = jnp.where((lane & 8) == 8, -1.0, 1.0)
    for block in range(8):
        base = 16 * (block // 2)
        above = block % 2 == 1
        even_p, even_q = even[base : base + 8], even[base + 8 : base + 16]
        odd_p, odd_q = odd[base : base + 8], odd[base + 8 : base + 16]
        even_row = even_p - even_q if above else even_p + even_q
        odd_row = odd_p + odd_q if above else odd_p - odd_q
        less, more = even_row - odd_row, even_row + odd_row
        for index, one, two, reverse in (
            (8 + block, less, more, not above),
            (7 - block, more, less, above),
        ):
            values = paired(one, near, reverse) + sign * paired(two, near ^ 8, reverse)
            piece = index // 4
            slot = ((piece & 1) ^ core) * 2 + ((piece >> 1) ^ far)
            place = pl.multiple_of(slot * 32 + 8 * (index % 4), 8)
            image_ref[pl.ds(place, 8), :] = values


SMALL = pltpu.CompilerParams(vmem_limit_bytes=8 << 20)
VMEM = pl.BlockSpec(memory_space=pltpu.VMEM)


def body(total, plane, visibilities, weights, uv_cells, flags, plan, beam, facets):
    arguments = (visibilities, weights, uv_cells, flags, plan[None], beam, facets)
    note = jax.ShapeDtypeStruct((16 + 2 * plane, LANES), jnp.float32)
    packed, mine, other = pl.pallas_call(
        pack_kernel,
        out_shape=(jax.ShapeDtypeStruct((plane, 16, LANES), jnp.float32), note, note),
        in_specs=[pl.BlockSpec(memory_space=pltpu.HBM)] * 7,
        out_specs=(VMEM, VMEM, VMEM),
        scratch_shapes=[pltpu.VMEM(each.shape, each.dtype) for each in arguments]
        + [
            pltpu.VMEM((8, weights.shape[1]), jnp.float32),
            pltpu.SemaphoreType.DMA((len(arguments),)),
        ],
        compiler_params=SMALL,
    )(*(pltpu.with_memory_space_constraint(each, pltpu.HBM) for each in arguments))
    across = [(i, i ^ 65) for i in range(4 * 2 * plane)]
    other = lax.ppermute(other, ("freq", "facet"), across)
    groups = [list(range(side, 2 * plane, 2)) for side in range(2)]
    near = lax.all_to_all(packed, "facet", 0, 0, axis_index_groups=groups)
    near = near.reshape(plane * 16, LANES)
    buffers = [
        pltpu.VMEM((2, 64, LANES), jnp.float32),
        pltpu.VMEM((2, 64, LANES), jnp.float32),
        pltpu.VMEM((16, 8, LANES), jnp.float32),
        pltpu.VMEM((8, 8, LANES), jnp.float32),
    ]
    scratch = buffers * 2
    cost = pl.CostEstimate(
        flops=2 * 2 * HALF * P_SIZE * 2 * plane * KEEP, bytes_accessed=1 << 18, transcendentals=0
    )

    def image(swap, note):
        return pl.pallas_call(
            functools.partial(image_kernel, 2.0 / math.sqrt(total), swap),
            out_shape=jax.ShapeDtypeStruct((P_SIZE, P_SIZE), jnp.float32),
            in_specs=[VMEM] * 2,
            out_specs=VMEM,
            scratch_shapes=scratch,
            compiler_params=SMALL,
            cost_estimate=cost,
        )(note, near)

    joined = lax.ppermute(image(1, other), ("freq", "facet"), across)
    joined = joined + image(0, mine)
    half = joined[:HALF] + lax.ppermute(joined[HALF:], "freq", [(i, i ^ 1) for i in range(4)])
    return (half[:32] + lax.ppermute(half[32:], "freq", [(i, i ^ 2) for i in range(4)]))[None]


def solution(mesh):
    in_specs = (
        P("facet", None, "freq"),
        P("facet", "freq"),
        P("facet", None, "freq"),
        P("facet", "freq"),
        P(),
        P("facet", None),
        P("facet", None),
    )
    total = 64 * 2048
    return jax.shard_map(
        functools.partial(body, total, mesh.shape["facet"] // 2),
        mesh=mesh,
        in_specs=in_specs,
        out_specs=P("facet", "freq", None),
        check_vma=False,
    )
```

```python
import functools
import math

import jax
import jax.numpy as jnp
from jax import lax
from jax.experimental import pallas as pl
from jax.experimental.pallas import tpu as pltpu
from jax.sharding import PartitionSpec as P


P_SIZE = 128
IMG = 32768
KEEP = 256
LANES = 128
HALF = P_SIZE // 2


def lane_prefix(flags):
    rows = lax.broadcasted_iota(jnp.int32, (LANES, LANES), 0)
    columns = lax.broadcasted_iota(jnp.int32, (LANES, LANES), 1)
    earlier = (rows < columns).astype(jnp.bfloat16)
    running = jnp.zeros((flags.shape[0], 1), jnp.float32)
    parts = []
    for start in range(0, flags.shape[1], LANES):
        piece = flags[:, start : start + LANES]
        inside = jnp.dot(piece.astype(jnp.bfloat16), earlier, preferred_element_type=jnp.float32)
        parts.append(inside + running)
        running = running + jnp.sum(piece, axis=1, keepdims=True)
    return jnp.concatenate(parts, axis=1)


def pack_kernel(
    vis_in, weight_in, uv_in, flag_in, plan_in, beam_in, facet_in,
    out_ref, mine_ref, other_ref,
    vis_ref, weight_ref, uv_ref, flag_ref, plan_ref, beam_ref, facet_ref, data_ref, arrived,
):
    copies = [
        pltpu.make_async_copy(source, target, arrived.at[index])
        for index, (source, target) in enumerate(
            (
                (flag_in, flag_ref), (vis_in, vis_ref), (weight_in, weight_ref), (uv_in, uv_ref),
                (plan_in, plan_ref), (beam_in, beam_ref), (facet_in, facet_ref),
            )
        )
    ]
    for copy in copies:
        copy.start()
    for copy in copies:
        copy.wait()
    rows = weight_ref.shape[1]
    flags = flag_ref[...].astype(jnp.float32)
    weights = weight_ref[...]
    data_ref[0:2, :] = vis_ref[:, 0, :] * weights
    data_ref[2:4, :] = vis_ref[:, 1, :] * weights
    data_ref[4:6, :] = uv_ref[:, 0, :].astype(jnp.float32)
    data_ref[6:8, :] = uv_ref[:, 1, :].astype(jnp.float32)
    data = data_ref[...]
    high = data.astype(jnp.bfloat16).astype(jnp.float32)
    rest = data - high
    middle = rest.astype(jnp.bfloat16).astype(jnp.float32)
    low = rest - middle
    pieces = jnp.concatenate([high, middle, low], axis=0).astype(jnp.bfloat16)
    spot = jnp.where(flags > 0.0, lane_prefix(flags), -1.0).astype(jnp.int32)
    target = lax.broadcasted_iota(jnp.int32, (KEEP, rows), 0)
    packed = []
    for block in range(2):
        chosen = (target == spot[block : block + 1, :]).astype(jnp.float32).astype(jnp.bfloat16)
        moved = lax.dot_general(
            pieces, chosen, (((1,), (1,)), ((), ())), preferred_element_type=jnp.float32
        )
        packed.append(moved[0:8] + moved[8:16] + moved[16:24])
    parity = lax.broadcasted_iota(jnp.int32, packed[0].shape, 0) & 1
    result = jnp.where(parity == 0, packed[0], packed[1])
    plane = out_ref.shape[0]
    for peer in range(plane):
        out_ref[peer, 0:8, :] = result[:, :LANES]
        out_ref[peer, 8:16, :] = result[:, LANES:]
    side = lax.axis_index("facet") & 1
    shape = (plane, plan_ref.shape[1])
    for which, note_ref in ((0, mine_ref), (1, other_ref)):
        for axis in range(2):
            centre = 2 * (facet_ref[0:1, axis : axis + 1] * P_SIZE - IMG // 2) + (P_SIZE - 1)
            note_ref[8 * axis : 8 * axis + 8, :] = jnp.broadcast_to(
                centre.astype(jnp.float32), (8, LANES)
            )
        for member in range(2):
            block = 4 * lax.broadcasted_iota(jnp.int32, shape, 0) + 2 * (side ^ which) + member
            matches = plan_ref[...] == block
            gain = jnp.sum(jnp.where(matches, beam_ref[...], 0.0), axis=1, keepdims=True)
            first = 16 + member * plane
            note_ref[first : first + plane, :] = jnp.broadcast_to(gain, (plane, LANES))


def doubled(sine, cosine):
    twice = sine + sine
    return twice * cosine, 1.0 - twice * sine


def sine_cosine(turns):
    x = ((turns << 16) >> 16).astype(jnp.float32) * (2.0 * math.pi / 65536.0 / 4.0)
    y = x * x
    sine = x * (1.0 + y * (-1.0 / 6 + y * (1.0 / 120 + y * (-1.0 / 5040 + y * (1.0 / 362880)))))
    cosine = 1.0 + y * (-0.5 + y * (1.0 / 24 + y * (-1.0 / 720 + y * (1.0 / 40320))))
    return doubled(*doubled(sine, cosine))


def half_steps(sine, cosine, count):
    twice = 4.0 * cosine * cosine - 2.0
    sines, cosines = [sine], [cosine]
    before_sine, before_cosine = -sine, cosine
    for _ in range(count - 1):
        sines.append(twice * sines[-1] - before_sine)
        cosines.append(twice * cosines[-1] - before_cosine)
        before_sine, before_cosine = sines[-2], cosines[-2]
    return sines, cosines


def chunk_tables(outer, fine, count, chunk):
    cosine, sine = fine[0, pl.ds(8 * chunk, 8), :], fine[1, pl.ds(8 * chunk, 8), :]
    first, second = [], []
    for far in range(count):
        x = jnp.broadcast_to(outer[2 * far, pl.ds(chunk, 1), :], (8, LANES))
        y = jnp.broadcast_to(outer[2 * far + 1, pl.ds(chunk, 1), :], (8, LANES))
        first += [x * cosine, y * sine]
        second += [y * cosine, x * sine]
    return (
        jnp.concatenate(first, axis=0).astype(jnp.bfloat16),
        jnp.concatenate(second, axis=0).astype(jnp.bfloat16),
    )


def prepare(note_ref, data_ref, step, half, buffers):
    fine_v, fine_u, outer, coarse = buffers
    column = note_ref[0:8, :].astype(jnp.int32)
    row = note_ref[8:16, :].astype(jnp.int32)
    tile = step >> 1
    member = step & 1
    place = 16 + member * (data_ref.shape[0] // 16) + tile * 8
    gain = note_ref[pl.ds(pl.multiple_of(place, 8), 8), :]
    first = tile * 128 + 8 * half + member
    real, imag, u, v = (
        data_ref[pl.ds(first + 2 * kind, 8, stride=16), :] for kind in range(4)
    )
    u = u.astype(jnp.int32)
    v = v.astype(jnp.int32)
    real = real * gain
    imag = imag * gain
    sine, cosine = sine_cosine(u * column + v * row)
    centre_real = real * cosine - imag * sine
    centre_imag = real * sine + imag * cosine
    near_v = sine_cosine(v)
    near_u = sine_cosine(u)
    for near, fine in ((near_v, fine_v), (near_u, fine_u)):
        sines, cosines = half_steps(*near, 8)
        for tau in range(8):
            fine[0, pl.ds(tau, 8, stride=8), :] = cosines[tau]
            fine[1, pl.ds(tau, 8, stride=8), :] = sines[tau]
    for _ in range(4):
        near_v = doubled(*near_v)
        near_u = doubled(*near_u)
    sines, cosines = half_steps(*near_u, 4)
    for far in range(4):
        coarse[2 * far] = cosines[far]
        coarse[2 * far + 1] = sines[far]
    sines, cosines = half_steps(*near_v, 4)
    for far in range(4):
        rc, isn = centre_real * cosines[far], centre_imag * sines[far]
        ic, rs = centre_imag * cosines[far], centre_real * sines[far]
        above, below = 4 + far, 3 - far
        outer[2 * above] = rc - isn
        outer[2 * above + 1] = ic + rs
        outer[2 * below] = rc + isn
        outer[2 * below + 1] = ic - rs


def accumulate(buffers, sums):
    fine_v, fine_u, outer, coarse = buffers
    even, odd = sums
    for pair in range(4):
        tables = [
            chunk_tables(coarse, fine_u, 4, chunk) + chunk_tables(outer, fine_v, 8, chunk)
            for chunk in (2 * pair, 2 * pair + 1)
        ]
        c, s, a, b = (jnp.concatenate(table, axis=1) for table in zip(*tables))
        contract = (((1,), (1,)), ((), ()))
        even = even + lax.dot_general(c, a, contract, preferred_element_type=jnp.float32)
        odd = odd + lax.dot_general(s, b, contract, preferred_element_type=jnp.float32)
    return even, odd


def paired(values, source, reverse):
    values = jnp.take_along_axis(values, source, axis=1)
    if reverse:
        values = jnp.take_along_axis(
            values, 7 - lax.broadcasted_iota(jnp.int32, values.shape, 0), axis=0
        )
    return values


def sum_blocks(note_ref, data_ref, scratch, sums, begin, end):
    buffers = (scratch[0:4], scratch[4:8])
    prepare(note_ref, data_ref, begin, 0, buffers[0])

    def advance(step, sums):
        prepare(note_ref, data_ref, step, 1, buffers[1])
        sums = accumulate(buffers[0], sums)
        prepare(note_ref, data_ref, jnp.minimum(step + 1, end - 1), 0, buffers[0])
        return accumulate(buffers[1], sums)

    return lax.fori_loop(begin, end, advance, sums)


def part_kernel(begin, end, note_ref, data_ref, even_ref, odd_ref, *scratch):
    zero = jnp.zeros((HALF, P_SIZE), jnp.float32)
    even, odd = sum_blocks(note_ref, data_ref, scratch, (zero, zero), begin, end)
    even_ref[...] = even
    odd_ref[...] = odd


def image_kernel(scale, swap, begin, end, note_ref, data_ref, *rest):
    if begin:
        even_ref, odd_ref, *rest = rest
        sums = (even_ref[...], odd_ref[...])
    else:
        sums = (jnp.zeros((HALF, P_SIZE), jnp.float32),) * 2
    keep_ref, send_ref, image_ref, *scratch = rest
    even, odd = sum_blocks(note_ref, data_ref, scratch, sums, begin, end)
    even, odd = even * scale, odd * scale
    core = lax.axis_index("freq") & 1
    far = (lax.axis_index("freq") >> 1) ^ swap
    lane = lax.broadcasted_iota(jnp.int32, (8, P_SIZE), 1)
    near = jnp.where((lane & 8) == 8, lane ^ 8, lane ^ 7)
    sign = jnp.where((lane & 8) == 8, -1.0, 1.0)
    for block in range(8):
        base = 16 * (block // 2)
        above = block % 2 == 1
        even_p, even_q = even[base : base + 8], even[base + 8 : base + 16]
        odd_p, odd_q = odd[base : base + 8], odd[base + 8 : base + 16]
        even_row = even_p - even_q if above else even_p + even_q
        odd_row = odd_p + odd_q if above else odd_p - odd_q
        less, more = even_row - odd_row, even_row + odd_row
        for index, one, two, reverse in (
            (8 + block, less, more, not above),
            (7 - block, more, less, above),
        ):
            values = paired(one, near, reverse) + sign * paired(two, near ^ 8, reverse)
            piece = index // 4
            slot = ((piece & 1) ^ core) * 2 + ((piece >> 1) ^ far)
            place = pl.multiple_of(slot * 32 + 8 * (index % 4), 8)
            image_ref[pl.ds(place, 8), :] = values
    keep_ref[...] = image_ref[0:HALF, :]
    send_ref[...] = image_ref[HALF:, :]


SMALL = pltpu.CompilerParams(vmem_limit_bytes=8 << 20)
VMEM = pl.BlockSpec(memory_space=pltpu.VMEM)


def body(total, plane, visibilities, weights, uv_cells, flags, plan, beam, facets):
    arguments = (visibilities, weights, uv_cells, flags, plan[None], beam, facets)
    note = jax.ShapeDtypeStruct((16 + 2 * plane, LANES), jnp.float32)
    packed, mine, other = pl.pallas_call(
        pack_kernel,
        out_shape=(jax.ShapeDtypeStruct((plane, 16, LANES), jnp.float32), note, note),
        in_specs=[pl.BlockSpec(memory_space=pltpu.HBM)] * 7,
        out_specs=(VMEM, VMEM, VMEM),
        scratch_shapes=[pltpu.VMEM(each.shape, each.dtype) for each in arguments]
        + [
            pltpu.VMEM((8, weights.shape[1]), jnp.float32),
            pltpu.SemaphoreType.DMA((len(arguments),)),
        ],
        compiler_params=SMALL,
    )(*(pltpu.with_memory_space_constraint(each, pltpu.HBM) for each in arguments))
    across = [(i, i ^ 65) for i in range(4 * 2 * plane)]
    other = lax.ppermute(other, ("freq", "facet"), across)
    groups = [list(range(side, 2 * plane, 2)) for side in range(2)]
    near = lax.all_to_all(packed, "facet", 0, 0, axis_index_groups=groups)
    near = near.reshape(plane * 16, LANES)
    buffers = [
        pltpu.VMEM((2, 64, LANES), jnp.float32),
        pltpu.VMEM((2, 64, LANES), jnp.float32),
        pltpu.VMEM((16, 8, LANES), jnp.float32),
        pltpu.VMEM((8, 8, LANES), jnp.float32),
    ]
    scratch = buffers * 2
    scale = 2.0 / math.sqrt(total)
    steps = plane // 4
    rows = jax.ShapeDtypeStruct((HALF, P_SIZE), jnp.float32)

    def call(kernel, count, operands, scratch):
        cost = pl.CostEstimate(
            flops=count * 2 * 2 * HALF * P_SIZE * 16 * KEEP, bytes_accessed=1 << 18, transcendentals=0
        )
        return pl.pallas_call(
            kernel,
            out_shape=(rows, rows),
            in_specs=[VMEM] * len(operands),
            out_specs=(VMEM, VMEM),
            scratch_shapes=scratch,
            compiler_params=SMALL,
            cost_estimate=cost,
        )(*operands)

    whole = [pltpu.VMEM((P_SIZE, P_SIZE), jnp.float32)]
    cores = [(i, i ^ 1) for i in range(4)]
    keep, send = call(
        functools.partial(image_kernel, scale, 1, 0, steps), steps, (other, near), whole + scratch
    )
    middle = steps // 2
    sums = call(functools.partial(part_kernel, 0, middle), middle, (mine, near), scratch)
    visitor, sums = lax.optimization_barrier(
        (keep + lax.ppermute(send, "freq", cores), tuple(sums))
    )
    visitor = lax.ppermute(visitor, ("freq", "facet"), across)
    keep, send = call(
        functools.partial(image_kernel, scale, 0, middle, steps),
        steps - middle, (mine, near, *sums), whole + scratch,
    )
    half = keep + lax.ppermute(send, "freq", cores) + visitor
    return (half[:32] + lax.ppermute(half[32:], "freq", [(i, i ^ 2) for i in range(4)]))[None]


def solution(mesh):
    in_specs = (
        P("facet", None, "freq"),
        P("facet", "freq"),
        P("facet", None, "freq"),
        P("facet", "freq"),
        P(),
        P("facet", None),
        P("facet", None),
    )
    total = 64 * 2048
    return jax.shard_map(
        functools.partial(body, total, mesh.shape["facet"] // 2),
        mesh=mesh,
        in_specs=in_specs,
        out_specs=P("facet", "freq", None),
        check_vma=False,
    )
```

```python
import functools
import math

import jax
import jax.numpy as jnp
from jax import lax
from jax.experimental import pallas as pl
from jax.experimental.pallas import tpu as pltpu
from jax.sharding import PartitionSpec as P

P_SIZE = 128
IMG = 32768
KEEP = 256
LANES = 128
HALF = P_SIZE // 2


def lane_prefix(flags):
    rows = lax.broadcasted_iota(jnp.int32, (LANES, LANES), 0)
    columns = lax.broadcasted_iota(jnp.int32, (LANES, LANES), 1)
    earlier = (rows < columns).astype(jnp.bfloat16)
    running = jnp.zeros((flags.shape[0], 1), jnp.float32)
    parts = []
    for start in range(0, flags.shape[1], LANES):
        piece = flags[:, start : start + LANES]
        inside = jnp.dot(piece.astype(jnp.bfloat16), earlier, preferred_element_type=jnp.float32)
        parts.append(inside + running)
        running = running + jnp.sum(piece, axis=1, keepdims=True)
    return jnp.concatenate(parts, axis=1)


def pack_kernel(
    vis_in, weight_in, uv_in, flag_in, plan_in, beam_in, facet_in,
    out_ref, mine_ref, other_ref,
    vis_ref, weight_ref, uv_ref, flag_ref, plan_ref, beam_ref, facet_ref, data_ref, arrived,
):
    copies = [
        pltpu.make_async_copy(source, target, arrived.at[index])
        for index, (source, target) in enumerate(
            (
                (flag_in, flag_ref), (vis_in, vis_ref), (weight_in, weight_ref), (uv_in, uv_ref),
                (plan_in, plan_ref), (beam_in, beam_ref), (facet_in, facet_ref),
            )
        )
    ]
    for copy in copies:
        copy.start()
    for copy in copies:
        copy.wait()
    rows = weight_ref.shape[1]
    flags = flag_ref[...].astype(jnp.float32)
    weights = weight_ref[...]
    data_ref[0:2, :] = vis_ref[:, 0, :] * weights
    data_ref[2:4, :] = vis_ref[:, 1, :] * weights
    data_ref[4:6, :] = uv_ref[:, 0, :].astype(jnp.float32)
    data_ref[6:8, :] = uv_ref[:, 1, :].astype(jnp.float32)
    data = data_ref[...]
    high = data.astype(jnp.bfloat16).astype(jnp.float32)
    rest = data - high
    middle = rest.astype(jnp.bfloat16).astype(jnp.float32)
    low = rest - middle
    pieces = jnp.concatenate([high, middle, low], axis=0).astype(jnp.bfloat16)
    spot = jnp.where(flags > 0.0, lane_prefix(flags), -1.0).astype(jnp.int32)
    target = lax.broadcasted_iota(jnp.int32, (KEEP, rows), 0)
    packed = []
    for block in range(2):
        chosen = (target == spot[block : block + 1, :]).astype(jnp.float32).astype(jnp.bfloat16)
        moved = lax.dot_general(
            pieces, chosen, (((1,), (1,)), ((), ())), preferred_element_type=jnp.float32
        )
        packed.append(moved[0:8] + moved[8:16] + moved[16:24])
    parity = lax.broadcasted_iota(jnp.int32, packed[0].shape, 0) & 1
    result = jnp.where(parity == 0, packed[0], packed[1])
    plane = out_ref.shape[0]
    for peer in range(plane):
        out_ref[peer, 0:8, :] = result[:, :LANES]
        out_ref[peer, 8:16, :] = result[:, LANES:]
    side = lax.axis_index("facet") & 1
    shape = (plane, plan_ref.shape[1])
    for which, note_ref in ((0, mine_ref), (1, other_ref)):
        for axis in range(2):
            centre = 2 * (facet_ref[0:1, axis : axis + 1] * P_SIZE - IMG // 2) + (P_SIZE - 1)
            note_ref[8 * axis : 8 * axis + 8, :] = jnp.broadcast_to(
                centre.astype(jnp.float32), (8, LANES)
            )
        for member in range(2):
            block = 4 * lax.broadcasted_iota(jnp.int32, shape, 0) + 2 * (side ^ which) + member
            matches = plan_ref[...] == block
            gain = jnp.sum(jnp.where(matches, beam_ref[...], 0.0), axis=1, keepdims=True)
            first = 16 + member * plane
            note_ref[first : first + plane, :] = jnp.broadcast_to(gain, (plane, LANES))


def doubled(sine, cosine):
    twice = sine + sine
    return twice * cosine, 1.0 - twice * sine


def sine_cosine(turns):
    x = ((turns << 16) >> 16).astype(jnp.float32) * (2.0 * math.pi / 65536.0 / 4.0)
    y = x * x
    sine = x * (1.0 + y * (-1.0 / 6 + y * (1.0 / 120 + y * (-1.0 / 5040 + y * (1.0 / 362880)))))
    cosine = 1.0 + y * (-0.5 + y * (1.0 / 24 + y * (-1.0 / 720 + y * (1.0 / 40320))))
    return doubled(*doubled(sine, cosine))


def half_steps(sine, cosine, count):
    twice = 4.0 * cosine * cosine - 2.0
    sines, cosines = [sine], [cosine]
    before_sine, before_cosine = -sine, cosine
    for _ in range(count - 1):
        sines.append(twice * sines[-1] - before_sine)
        cosines.append(twice * cosines[-1] - before_cosine)
        before_sine, before_cosine = sines[-2], cosines[-2]
    return sines, cosines


def chunk_tables(outer, fine, count, chunk):
    cosine, sine = fine[0, pl.ds(8 * chunk, 8), :], fine[1, pl.ds(8 * chunk, 8), :]
    first, second = [], []
    for far in range(count):
        x = jnp.broadcast_to(outer[2 * far, pl.ds(chunk, 1), :], (8, LANES))
        y = jnp.broadcast_to(outer[2 * far + 1, pl.ds(chunk, 1), :], (8, LANES))
        first += [x * cosine, y * sine]
        second += [y * cosine, x * sine]
    return (
        jnp.concatenate(first, axis=0).astype(jnp.bfloat16),
        jnp.concatenate(second, axis=0).astype(jnp.bfloat16),
    )


def prepare(notes, data_ref, step, half, buffers):
    fine_v, fine_u, coarse, *outers = buffers
    tile = step >> 1
    member = step & 1
    place = pl.multiple_of(16 + member * (data_ref.shape[0] // 16) + tile * 8, 8)
    first = tile * 128 + 8 * half + member
    real, imag, u, v = (
        data_ref[pl.ds(first + 2 * kind, 8, stride=16), :] for kind in range(4)
    )
    u = u.astype(jnp.int32)
    v = v.astype(jnp.int32)
    near_v = sine_cosine(v)
    near_u = sine_cosine(u)
    for near, fine in ((near_v, fine_v), (near_u, fine_u)):
        sines, cosines = half_steps(*near, 8)
        for tau in range(8):
            fine[0, pl.ds(tau, 8, stride=8), :] = cosines[tau]
            fine[1, pl.ds(tau, 8, stride=8), :] = sines[tau]
    for _ in range(4):
        near_v = doubled(*near_v)
        near_u = doubled(*near_u)
    sines, cosines = half_steps(*near_u, 4)
    for far in range(4):
        coarse[2 * far] = cosines[far]
        coarse[2 * far + 1] = sines[far]
    sines, cosines = half_steps(*near_v, 4)
    for note_ref, outer in zip(notes, outers):
        column = note_ref[0:8, :].astype(jnp.int32)
        row = note_ref[8:16, :].astype(jnp.int32)
        gain = note_ref[pl.ds(place, 8), :]
        sine, cosine = sine_cosine(u * column + v * row)
        sine, cosine = sine * gain, cosine * gain
        centre_real = real * cosine - imag * sine
        centre_imag = real * sine + imag * cosine
        for far in range(4):
            rc, isn = centre_real * cosines[far], centre_imag * sines[far]
            ic, rs = centre_imag * cosines[far], centre_real * sines[far]
            above, below = 4 + far, 3 - far
            outer[2 * above] = rc - isn
            outer[2 * above + 1] = ic + rs
            outer[2 * below] = rc + isn
            outer[2 * below + 1] = ic - rs


def accumulate(buffers, sums):
    fine_v, fine_u, coarse, *outers = buffers
    even, odd = sums
    for pair in range(4):
        left, right = [], []
        for chunk in (2 * pair, 2 * pair + 1):
            left.append(chunk_tables(coarse, fine_u, 4, chunk))
            facets = [chunk_tables(outer, fine_v, 8, chunk) for outer in outers]
            right.append(tuple(jnp.concatenate(table, axis=0) for table in zip(*facets)))
        c, s = (jnp.concatenate(table, axis=1) for table in zip(*left))
        a, b = (jnp.concatenate(table, axis=1) for table in zip(*right))
        contract = (((1,), (1,)), ((), ()))
        even = even + lax.dot_general(c, a, contract, preferred_element_type=jnp.float32)
        odd = odd + lax.dot_general(s, b, contract, preferred_element_type=jnp.float32)
    return even, odd


def paired(values, source, reverse):
    values = jnp.take_along_axis(values, source, axis=1)
    if reverse:
        values = jnp.take_along_axis(
            values, 7 - lax.broadcasted_iota(jnp.int32, values.shape, 0), axis=0
        )
    return values


def image_kernel(scale, mine_ref, other_ref, data_ref, keep_ref, send_ref, image_ref, *scratch):
    notes = (mine_ref, other_ref)
    buffers = (scratch[0:5], scratch[5:10])
    steps = data_ref.shape[0] // 64
    prepare(notes, data_ref, 0, 0, buffers[0])

    def advance(step, sums):
        prepare(notes, data_ref, step, 1, buffers[1])
        sums = accumulate(buffers[0], sums)
        prepare(notes, data_ref, (step + 1) & (steps - 1), 0, buffers[0])
        return accumulate(buffers[1], sums)

    zero = jnp.zeros((HALF, 2 * P_SIZE), jnp.float32)
    evens, odds = lax.fori_loop(0, steps, advance, (zero, zero))
    core = lax.axis_index("freq") & 1
    far = lax.axis_index("freq") >> 1
    lane = lax.broadcasted_iota(jnp.int32, (8, P_SIZE), 1)
    near = jnp.where((lane & 8) == 8, lane ^ 8, lane ^ 7)
    sign = jnp.where((lane & 8) == 8, -scale, scale)
    for facet in range(2):
        columns = slice(facet * P_SIZE, (facet + 1) * P_SIZE)
        even, odd = evens[:, columns], odds[:, columns]
        for block in range(8):
            base = 16 * (block // 2)
            above = block % 2 == 1
            even_p, even_q = even[base : base + 8], even[base + 8 : base + 16]
            odd_p, odd_q = odd[base : base + 8], odd[base + 8 : base + 16]
            even_row = even_p - even_q if above else even_p + even_q
            odd_row = odd_p + odd_q if above else odd_p - odd_q
            less, more = even_row - odd_row, even_row + odd_row
            for index, one, two, reverse in (
                (8 + block, less, more, not above),
                (7 - block, more, less, above),
            ):
                values = scale * paired(one, near, reverse) + sign * paired(two, near ^ 8, reverse)
                piece = index // 4
                slot = ((piece & 1) ^ core) * 4 + 2 * facet + ((piece >> 1) ^ far)
                place = pl.multiple_of(slot * 32 + 8 * (index % 4), 8)
                image_ref[pl.ds(place, 8), :] = values
    keep_ref[...] = image_ref[0:P_SIZE, :]
    send_ref[...] = image_ref[P_SIZE:, :]


SMALL = pltpu.CompilerParams(vmem_limit_bytes=8 << 20)
VMEM = pl.BlockSpec(memory_space=pltpu.VMEM)


def body(total, plane, visibilities, weights, uv_cells, flags, plan, beam, facets):
    arguments = (visibilities, weights, uv_cells, flags, plan[None], beam, facets)
    note = jax.ShapeDtypeStruct((16 + 2 * plane, LANES), jnp.float32)
    packed, mine, other = pl.pallas_call(
        pack_kernel,
        out_shape=(jax.ShapeDtypeStruct((plane, 16, LANES), jnp.float32), note, note),
        in_specs=[pl.BlockSpec(memory_space=pltpu.HBM)] * 7,
        out_specs=(VMEM, VMEM, VMEM),
        scratch_shapes=[pltpu.VMEM(each.shape, each.dtype) for each in arguments]
        + [
            pltpu.VMEM((8, weights.shape[1]), jnp.float32),
            pltpu.SemaphoreType.DMA((len(arguments),)),
        ],
        compiler_params=SMALL,
    )(*(pltpu.with_memory_space_constraint(each, pltpu.HBM) for each in arguments))
    across = [(i, i ^ 65) for i in range(4 * 2 * plane)]
    other = lax.ppermute(other, ("freq", "facet"), across)
    groups = [list(range(side, 2 * plane, 2)) for side in range(2)]
    near = lax.all_to_all(packed, "facet", 0, 0, axis_index_groups=groups)
    near = near.reshape(plane * 16, LANES)
    outer = pltpu.VMEM((16, 8, LANES), jnp.float32)
    buffers = [
        pltpu.VMEM((2, 64, LANES), jnp.float32),
        pltpu.VMEM((2, 64, LANES), jnp.float32),
        pltpu.VMEM((8, 8, LANES), jnp.float32),
        outer,
        outer,
    ]
    image = jax.ShapeDtypeStruct((P_SIZE, P_SIZE), jnp.float32)
    keep, send = pl.pallas_call(
        functools.partial(image_kernel, 2.0 / math.sqrt(total)),
        out_shape=(image, image),
        in_specs=[VMEM] * 3,
        out_specs=(VMEM, VMEM),
        scratch_shapes=[pltpu.VMEM((2 * P_SIZE, P_SIZE), jnp.float32)] + buffers * 2,
        compiler_params=SMALL,
    )(mine, other, near)
    half = keep + lax.ppermute(send, "freq", [(i, i ^ 1) for i in range(4)])
    result = half[:32]
    for piece, partner in ((2, 1), (1, 64), (3, 65)):
        result = result + lax.ppermute(
            half[32 * piece : 32 * piece + 32],
            ("freq", "facet"),
            [(i, i ^ partner) for i in range(8 * plane)],
        )
    return result[None]


def solution(mesh):
    in_specs = (
        P("facet", None, "freq"),
        P("facet", "freq"),
        P("facet", None, "freq"),
        P("facet", "freq"),
        P(),
        P("facet", None),
        P("facet", None),
    )
    total = 64 * 2048
    return jax.shard_map(
        functools.partial(body, total, mesh.shape["facet"] // 2),
        mesh=mesh,
        in_specs=in_specs,
        out_specs=P("facet", "freq", None),
        check_vma=False,
    )
```

```python
import functools
import math

import jax
import jax.numpy as jnp
from jax import lax
from jax.experimental import pallas as pl
from jax.experimental.pallas import tpu as pltpu
from jax.sharding import PartitionSpec as P

P_SIZE = 128
IMG = 32768
KEEP = 256
LANES = 128
HALF = P_SIZE // 2


def lane_prefix(flags):
    rows = lax.broadcasted_iota(jnp.int32, (LANES, LANES), 0)
    columns = lax.broadcasted_iota(jnp.int32, (LANES, LANES), 1)
    earlier = (rows < columns).astype(jnp.bfloat16)
    running = jnp.zeros((flags.shape[0], 1), jnp.float32)
    parts = []
    for start in range(0, flags.shape[1], LANES):
        piece = flags[:, start : start + LANES]
        inside = jnp.dot(piece.astype(jnp.bfloat16), earlier, preferred_element_type=jnp.float32)
        parts.append(inside + running)
        running = running + jnp.sum(piece, axis=1, keepdims=True)
    return jnp.concatenate(parts, axis=1)


def pack_kernel(
    vis_in, weight_in, uv_in, flag_in, plan_in, beam_in, facet_in,
    out_ref, gain_ref, centre_ref,
    vis_ref, weight_ref, uv_ref, flag_ref, plan_ref, beam_ref, facet_ref, data_ref, arrived,
):
    copies = [
        pltpu.make_async_copy(source, target, arrived.at[index])
        for index, (source, target) in enumerate(
            (
                (flag_in, flag_ref), (vis_in, vis_ref), (weight_in, weight_ref), (uv_in, uv_ref),
                (plan_in, plan_ref), (beam_in, beam_ref), (facet_in, facet_ref),
            )
        )
    ]
    for copy in copies:
        copy.start()
    copies[0].wait()
    rows = weight_ref.shape[1]
    flags = flag_ref[...].astype(jnp.float32)
    spot = jnp.where(flags > 0.0, lane_prefix(flags), -1.0).astype(jnp.int32)
    for copy in copies[1:]:
        copy.wait()
    weights = weight_ref[...]
    data_ref[0:2, :] = vis_ref[:, 0, :] * weights
    data_ref[2:4, :] = vis_ref[:, 1, :] * weights
    data_ref[4:6, :] = uv_ref[:, 0, :].astype(jnp.float32)
    data_ref[6:8, :] = uv_ref[:, 1, :].astype(jnp.float32)
    data = data_ref[...]
    high = data.astype(jnp.bfloat16).astype(jnp.float32)
    rest = data - high
    middle = rest.astype(jnp.bfloat16).astype(jnp.float32)
    low = rest - middle
    pieces = jnp.concatenate([high, middle, low], axis=0).astype(jnp.bfloat16)
    target = lax.broadcasted_iota(jnp.int32, (KEEP, rows), 0)
    packed = []
    for block in range(2):
        chosen = (target == spot[block : block + 1, :]).astype(jnp.float32).astype(jnp.bfloat16)
        moved = lax.dot_general(
            pieces, chosen, (((1,), (1,)), ((), ())), preferred_element_type=jnp.float32
        )
        packed.append(moved[0:8] + moved[8:16] + moved[16:24])
    parity = lax.broadcasted_iota(jnp.int32, packed[0].shape, 0) & 1
    result = jnp.where(parity == 0, packed[0], packed[1])
    plane = out_ref.shape[0]
    for peer in range(plane):
        out_ref[peer, 0:8, :] = result[:, :LANES]
        out_ref[peer, 8:16, :] = result[:, LANES:]
    side = lax.axis_index("facet") & 1
    shape = (plane, plan_ref.shape[1])
    for which in range(2):
        for member in range(2):
            block = 4 * lax.broadcasted_iota(jnp.int32, shape, 0) + 2 * (side ^ which) + member
            matches = plan_ref[...] == block
            gain = jnp.sum(jnp.where(matches, beam_ref[...], 0.0), axis=1, keepdims=True)
            first = (2 * which + member) * plane
            gain_ref[first : first + plane, :] = jnp.broadcast_to(gain, (plane, LANES))
    for axis in range(2):
        centre = 2 * (facet_ref[0:1, axis : axis + 1] * P_SIZE - IMG // 2) + (P_SIZE - 1)
        centre_ref[8 * axis : 8 * axis + 8, :] = jnp.broadcast_to(centre, (8, LANES))


def doubled(sine, cosine):
    twice = sine + sine
    return twice * cosine, 1.0 - twice * sine


def sine_cosine(turns):
    x = ((turns << 16) >> 16).astype(jnp.float32) * (2.0 * math.pi / 65536.0 / 4.0)
    y = x * x
    sine = x * (1.0 + y * (-1.0 / 6 + y * (1.0 / 120 + y * (-1.0 / 5040 + y * (1.0 / 362880)))))
    cosine = 1.0 + y * (-0.5 + y * (1.0 / 24 + y * (-1.0 / 720 + y * (1.0 / 40320))))
    return doubled(*doubled(sine, cosine))


def half_steps(sine, cosine, count):
    twice = 4.0 * cosine * cosine - 2.0
    sines, cosines = [sine], [cosine]
    before_sine, before_cosine = -sine, cosine
    for _ in range(count - 1):
        sines.append(twice * sines[-1] - before_sine)
        cosines.append(twice * cosines[-1] - before_cosine)
        before_sine, before_cosine = sines[-2], cosines[-2]
    return sines, cosines


def chunk_tables(outer, fine, count, chunk):
    cosine, sine = fine[0, pl.ds(8 * chunk, 8), :], fine[1, pl.ds(8 * chunk, 8), :]
    first, second = [], []
    for far in range(count):
        x = jnp.broadcast_to(outer[2 * far, pl.ds(chunk, 1), :], (8, LANES))
        y = jnp.broadcast_to(outer[2 * far + 1, pl.ds(chunk, 1), :], (8, LANES))
        first += [x * cosine, y * sine]
        second += [y * cosine, x * sine]
    return (
        jnp.concatenate(first, axis=0).astype(jnp.bfloat16),
        jnp.concatenate(second, axis=0).astype(jnp.bfloat16),
    )


def prepare(which, centre_ref, data_ref, gain_ref, step, half, buffers):
    fine_v, fine_u, outer, coarse = buffers
    column, row = centre_ref[0:8, :], centre_ref[8:16, :]
    tile = step >> 1
    member = step & 1
    owners = gain_ref.shape[0] // 4
    gain = gain_ref[pl.ds(pl.multiple_of((2 * which + member) * owners + tile * 8, 8), 8), :]
    first = tile * 128 + 8 * half + member
    real, imag, u, v = (
        data_ref[pl.ds(first + 2 * kind, 8, stride=16), :] for kind in range(4)
    )
    u = u.astype(jnp.int32)
    v = v.astype(jnp.int32)
    real = real * gain
    imag = imag * gain
    sine, cosine = sine_cosine(u * column + v * row)
    centre_real = real * cosine - imag * sine
    centre_imag = real * sine + imag * cosine
    near_v = sine_cosine(v)
    near_u = sine_cosine(u)
    for near, fine in ((near_v, fine_v), (near_u, fine_u)):
        sines, cosines = half_steps(*near, 8)
        for tau in range(8):
            fine[0, pl.ds(tau, 8, stride=8), :] = cosines[tau]
            fine[1, pl.ds(tau, 8, stride=8), :] = sines[tau]
    for _ in range(4):
        near_v = doubled(*near_v)
        near_u = doubled(*near_u)
    sines, cosines = half_steps(*near_u, 4)
    for far in range(4):
        coarse[2 * far] = cosines[far]
        coarse[2 * far + 1] = sines[far]
    sines, cosines = half_steps(*near_v, 4)
    for far in range(4):
        rc, isn = centre_real * cosines[far], centre_imag * sines[far]
        ic, rs = centre_imag * cosines[far], centre_real * sines[far]
        above, below = 4 + far, 3 - far
        outer[2 * above] = rc - isn
        outer[2 * above + 1] = ic + rs
        outer[2 * below] = rc + isn
        outer[2 * below + 1] = ic - rs


def accumulate(buffers, sums):
    fine_v, fine_u, outer, coarse = buffers
    even, odd = sums
    for pair in range(4):
        tables = [
            chunk_tables(coarse, fine_u, 4, chunk) + chunk_tables(outer, fine_v, 8, chunk)
            for chunk in (2 * pair, 2 * pair + 1)
        ]
        c, s, a, b = (jnp.concatenate(table, axis=1) for table in zip(*tables))
        contract = (((1,), (1,)), ((), ()))
        even = even + lax.dot_general(c, a, contract, preferred_element_type=jnp.float32)
        odd = odd + lax.dot_general(s, b, contract, preferred_element_type=jnp.float32)
    return even, odd


def paired(values, source, reverse):
    values = jnp.take_along_axis(values, source, axis=1)
    if reverse:
        values = jnp.take_along_axis(
            values, 7 - lax.broadcasted_iota(jnp.int32, values.shape, 0), axis=0
        )
    return values


def sum_blocks(which, centre_ref, gain_ref, data_ref, scratch, sums):
    buffers = (scratch[0:4], scratch[4:8])
    source = (which, centre_ref, data_ref, gain_ref)
    steps = data_ref.shape[0] // 64
    groups = [(step, half) for step in range(steps) for half in range(2)]
    prepare(*source, *groups[0], buffers[0])
    for index in range(len(groups)):
        if index + 1 < len(groups):
            prepare(*source, *groups[index + 1], buffers[(index + 1) % 2])
        sums = accumulate(buffers[index % 2], sums)
    return sums


def first_kernel(centre_ref, gain_ref, data_ref, even_ref, odd_ref, *scratch):
    zero = jnp.zeros((HALF, P_SIZE), jnp.float32)
    even, odd = sum_blocks(0, centre_ref, gain_ref, data_ref, scratch, (zero, zero))
    even_ref[...] = even
    odd_ref[...] = odd


def last_kernel(
    scale, centre_ref, gain_ref, data_ref, even_ref, odd_ref, keep_ref, send_ref,
    order_ref, *scratch,
):
    even, odd = sum_blocks(
        1, centre_ref, gain_ref, data_ref, scratch, (even_ref[...], odd_ref[...])
    )
    even, odd = even * scale, odd * scale
    core = lax.axis_index("freq") & 1
    far = lax.axis_index("freq") >> 1
    lane = lax.broadcasted_iota(jnp.int32, (8, P_SIZE), 1)
    near = jnp.where((lane & 8) == 8, lane ^ 8, lane ^ 7)
    sign = jnp.where((lane & 8) == 8, -1.0, 1.0)
    for block in range(8):
        base = 16 * (block // 2)
        above = block % 2 == 1
        even_p, even_q = even[base : base + 8], even[base + 8 : base + 16]
        odd_p, odd_q = odd[base : base + 8], odd[base + 8 : base + 16]
        even_row = even_p - even_q if above else even_p + even_q
        odd_row = odd_p + odd_q if above else odd_p - odd_q
        less, more = even_row - odd_row, even_row + odd_row
        for index, one, two, reverse in (
            (8 + block, less, more, not above),
            (7 - block, more, less, above),
        ):
            values = paired(one, near, reverse) + sign * paired(two, near ^ 8, reverse)
            piece = index // 4
            slot = ((piece & 1) ^ core) * 2 + ((piece >> 1) ^ far)
            place = pl.multiple_of(slot * 32 + 8 * (index % 4), 8)
            order_ref[pl.ds(place, 8), :] = values
    keep_ref[...] = order_ref[0:HALF, :]
    send_ref[...] = order_ref[HALF:, :]


SMALL = pltpu.CompilerParams(vmem_limit_bytes=8 << 20)
VMEM = pl.BlockSpec(memory_space=pltpu.VMEM)


def body(total, plane, visibilities, weights, uv_cells, flags, plan, beam, facets):
    arguments = (visibilities, weights, uv_cells, flags, plan[None], beam, facets)
    packed, gains, centre = pl.pallas_call(
        pack_kernel,
        out_shape=(
            jax.ShapeDtypeStruct((plane, 16, LANES), jnp.float32),
            jax.ShapeDtypeStruct((4 * plane, LANES), jnp.float32),
            jax.ShapeDtypeStruct((16, LANES), jnp.int32),
        ),
        in_specs=[pl.BlockSpec(memory_space=pltpu.HBM)] * 7,
        out_specs=(VMEM, VMEM, VMEM),
        scratch_shapes=[pltpu.VMEM(each.shape, each.dtype) for each in arguments]
        + [
            pltpu.VMEM((8, weights.shape[1]), jnp.float32),
            pltpu.SemaphoreType.DMA((len(arguments),)),
        ],
        compiler_params=SMALL,
    )(*(pltpu.with_memory_space_constraint(each, pltpu.HBM) for each in arguments))
    groups = [list(range(side, 2 * plane, 2)) for side in range(2)]
    near = lax.all_to_all(packed, "facet", 0, 0, axis_index_groups=groups)
    near = near.reshape(plane * 16, LANES)
    far = lax.ppermute(near, "facet", [(i, i ^ 1) for i in range(2 * plane)])
    image = jax.ShapeDtypeStruct((HALF, P_SIZE), jnp.float32)
    buffers = [
        pltpu.VMEM((2, 64, LANES), jnp.float32),
        pltpu.VMEM((2, 64, LANES), jnp.float32),
        pltpu.VMEM((16, 8, LANES), jnp.float32),
        pltpu.VMEM((8, 8, LANES), jnp.float32),
    ]
    scratch = buffers * 2
    cost = pl.CostEstimate(
        flops=2 * 2 * HALF * P_SIZE * 2 * plane * KEEP, bytes_accessed=1 << 18, transcendentals=0
    )
    even, odd = pl.pallas_call(
        first_kernel,
        out_shape=(image, image),
        in_specs=[VMEM] * 3,
        out_specs=(VMEM, VMEM),
        scratch_shapes=scratch,
        compiler_params=SMALL,
        cost_estimate=cost,
    )(centre, gains, near)
    keep, send = pl.pallas_call(
        functools.partial(last_kernel, 2.0 / math.sqrt(total)),
        out_shape=(image, image),
        in_specs=[VMEM] * 5,
        out_specs=(VMEM, VMEM),
        scratch_shapes=[pltpu.VMEM((P_SIZE, P_SIZE), jnp.float32)] + scratch,
        compiler_params=SMALL,
        cost_estimate=cost,
    )(centre, gains, far, even, odd)
    half = keep + lax.ppermute(send, "freq", [(i, i ^ 1) for i in range(4)])
    return (half[:32] + lax.ppermute(half[32:], "freq", [(i, i ^ 2) for i in range(4)]))[None]


def solution(mesh):
    in_specs = (
        P("facet", None, "freq"),
        P("facet", "freq"),
        P("facet", None, "freq"),
        P("facet", "freq"),
        P(),
        P("facet", None),
        P("facet", None),
    )
    total = 64 * 2048
    return jax.shard_map(
        functools.partial(body, total, mesh.shape["facet"] // 2),
        mesh=mesh,
        in_specs=in_specs,
        out_specs=P("facet", "freq", None),
        check_vma=False,
    )
```

```python
import functools
import math

import jax
import jax.numpy as jnp
from jax import lax
from jax.experimental import pallas as pl
from jax.experimental.pallas import tpu as pltpu
from jax.sharding import PartitionSpec as P

P_SIZE = 128
IMG = 32768
KEEP = 256
LANES = 128
HALF = P_SIZE // 2


def lane_prefix(flags):
    rows = lax.broadcasted_iota(jnp.int32, (LANES, LANES), 0)
    columns = lax.broadcasted_iota(jnp.int32, (LANES, LANES), 1)
    earlier = (rows < columns).astype(jnp.bfloat16)
    running = jnp.zeros((flags.shape[0], 1), jnp.float32)
    parts = []
    for start in range(0, flags.shape[1], LANES):
        piece = flags[:, start : start + LANES]
        inside = jnp.dot(piece.astype(jnp.bfloat16), earlier, preferred_element_type=jnp.float32)
        parts.append(inside + running)
        running = running + jnp.sum(piece, axis=1, keepdims=True)
    return jnp.concatenate(parts, axis=1)


def pack_kernel(
    vis_in, weight_in, uv_in, flag_in, plan_in, beam_in, facet_in,
    out_ref, gain_ref, centre_ref,
    vis_ref, weight_ref, uv_ref, flag_ref, plan_ref, beam_ref, facet_ref, data_ref, arrived,
):
    copies = [
        pltpu.make_async_copy(source, target, arrived.at[index])
        for index, (source, target) in enumerate(
            (
                (flag_in, flag_ref), (vis_in, vis_ref), (weight_in, weight_ref), (uv_in, uv_ref),
                (plan_in, plan_ref), (beam_in, beam_ref), (facet_in, facet_ref),
            )
        )
    ]
    for copy in copies:
        copy.start()
    copies[0].wait()
    rows = weight_ref.shape[1]
    flags = flag_ref[...].astype(jnp.float32)
    spot = jnp.where(flags > 0.0, lane_prefix(flags), -1.0).astype(jnp.int32)
    for copy in copies[1:]:
        copy.wait()
    weights = weight_ref[...]
    data_ref[0:2, :] = vis_ref[:, 0, :] * weights
    data_ref[2:4, :] = vis_ref[:, 1, :] * weights
    data_ref[4:6, :] = uv_ref[:, 0, :].astype(jnp.float32)
    data_ref[6:8, :] = uv_ref[:, 1, :].astype(jnp.float32)
    data = data_ref[...]
    high = data.astype(jnp.bfloat16).astype(jnp.float32)
    rest = data - high
    middle = rest.astype(jnp.bfloat16).astype(jnp.float32)
    low = rest - middle
    pieces = jnp.concatenate([high, middle, low], axis=0).astype(jnp.bfloat16)
    target = lax.broadcasted_iota(jnp.int32, (KEEP, rows), 0)
    packed = []
    for block in range(2):
        chosen = (target == spot[block : block + 1, :]).astype(jnp.float32).astype(jnp.bfloat16)
        moved = lax.dot_general(
            pieces, chosen, (((1,), (1,)), ((), ())), preferred_element_type=jnp.float32
        )
        packed.append(moved[0:8] + moved[8:16] + moved[16:24])
    parity = lax.broadcasted_iota(jnp.int32, packed[0].shape, 0) & 1
    result = jnp.where(parity == 0, packed[0], packed[1])
    plane = out_ref.shape[0]
    for peer in range(plane):
        out_ref[peer, 0:8, :] = result[:, :LANES]
        out_ref[peer, 8:16, :] = result[:, LANES:]
    side = lax.axis_index("facet") & 1
    shape = (plane, plan_ref.shape[1])
    for which in range(2):
        for member in range(2):
            block = 4 * lax.broadcasted_iota(jnp.int32, shape, 0) + 2 * (side ^ which) + member
            matches = plan_ref[...] == block
            gain = jnp.sum(jnp.where(matches, beam_ref[...], 0.0), axis=1, keepdims=True)
            first = (2 * which + member) * plane
            gain_ref[first : first + plane, :] = jnp.broadcast_to(gain, (plane, LANES))
    for axis in range(2):
        centre = 2 * (facet_ref[0:1, axis : axis + 1] * P_SIZE - IMG // 2) + (P_SIZE - 1)
        centre_ref[8 * axis : 8 * axis + 8, :] = jnp.broadcast_to(centre, (8, LANES))


def doubled(sine, cosine):
    twice = sine + sine
    return twice * cosine, 1.0 - twice * sine


def sine_cosine(turns):
    x = ((turns << 16) >> 16).astype(jnp.float32) * (2.0 * math.pi / 65536.0 / 4.0)
    y = x * x
    sine = x * (1.0 + y * (-1.0 / 6 + y * (1.0 / 120 + y * (-1.0 / 5040 + y * (1.0 / 362880)))))
    cosine = 1.0 + y * (-0.5 + y * (1.0 / 24 + y * (-1.0 / 720 + y * (1.0 / 40320))))
    return doubled(*doubled(sine, cosine))


def half_steps(sine, cosine, count):
    twice = 4.0 * cosine * cosine - 2.0
    sines, cosines = [sine], [cosine]
    before_sine, before_cosine = -sine, cosine
    for _ in range(count - 1):
        sines.append(twice * sines[-1] - before_sine)
        cosines.append(twice * cosines[-1] - before_cosine)
        before_sine, before_cosine = sines[-2], cosines[-2]
    return sines, cosines


def chunk_tables(outer, fine, count, chunk):
    cosine, sine = fine[0, pl.ds(8 * chunk, 8), :], fine[1, pl.ds(8 * chunk, 8), :]
    first, second = [], []
    for far in range(count):
        x = jnp.broadcast_to(outer[2 * far, pl.ds(chunk, 1), :], (8, LANES))
        y = jnp.broadcast_to(outer[2 * far + 1, pl.ds(chunk, 1), :], (8, LANES))
        first += [x * cosine, y * sine]
        second += [y * cosine, x * sine]
    return (
        jnp.concatenate(first, axis=0).astype(jnp.bfloat16),
        jnp.concatenate(second, axis=0).astype(jnp.bfloat16),
    )


def prepare(which, centre_ref, data_ref, gain_ref, step, half, buffers):
    fine_v, fine_u, outer, coarse = buffers
    column, row = centre_ref[0:8, :], centre_ref[8:16, :]
    tile = step >> 1
    member = step & 1
    owners = gain_ref.shape[0] // 4
    gain = gain_ref[pl.ds(pl.multiple_of((2 * which + member) * owners + tile * 8, 8), 8), :]
    first = tile * 128 + 8 * half + member
    real, imag, u, v = (
        data_ref[pl.ds(first + 2 * kind, 8, stride=16), :] for kind in range(4)
    )
    u = u.astype(jnp.int32)
    v = v.astype(jnp.int32)
    real = real * gain
    imag = imag * gain
    sine, cosine = sine_cosine(u * column + v * row)
    centre_real = real * cosine - imag * sine
    centre_imag = real * sine + imag * cosine
    near_v = sine_cosine(v)
    near_u = sine_cosine(u)
    for near, fine in ((near_v, fine_v), (near_u, fine_u)):
        sines, cosines = half_steps(*near, 8)
        for tau in range(8):
            fine[0, pl.ds(tau, 8, stride=8), :] = cosines[tau]
            fine[1, pl.ds(tau, 8, stride=8), :] = sines[tau]
    for _ in range(4):
        near_v = doubled(*near_v)
        near_u = doubled(*near_u)
    sines, cosines = half_steps(*near_u, 4)
    for far in range(4):
        coarse[2 * far] = cosines[far]
        coarse[2 * far + 1] = sines[far]
    sines, cosines = half_steps(*near_v, 4)
    for far in range(4):
        rc, isn = centre_real * cosines[far], centre_imag * sines[far]
        ic, rs = centre_imag * cosines[far], centre_real * sines[far]
        above, below = 4 + far, 3 - far
        outer[2 * above] = rc - isn
        outer[2 * above + 1] = ic + rs
        outer[2 * below] = rc + isn
        outer[2 * below + 1] = ic - rs


def accumulate(buffers, sums):
    fine_v, fine_u, outer, coarse = buffers
    even, odd = sums
    for pair in range(4):
        tables = [
            chunk_tables(coarse, fine_u, 4, chunk) + chunk_tables(outer, fine_v, 8, chunk)
            for chunk in (2 * pair, 2 * pair + 1)
        ]
        c, s, a, b = (jnp.concatenate(table, axis=1) for table in zip(*tables))
        contract = (((1,), (1,)), ((), ()))
        even = even + lax.dot_general(c, a, contract, preferred_element_type=jnp.float32)
        odd = odd + lax.dot_general(s, b, contract, preferred_element_type=jnp.float32)
    return even, odd


def paired(values, source, reverse):
    values = jnp.take_along_axis(values, source, axis=1)
    if reverse:
        values = jnp.take_along_axis(
            values, 7 - lax.broadcasted_iota(jnp.int32, values.shape, 0), axis=0
        )
    return values


def sum_blocks(which, centre_ref, gain_ref, data_ref, scratch, sums):
    buffers = [scratch[4 * k : 4 * k + 4] for k in range(8)]
    source = (which, centre_ref, data_ref, gain_ref)
    steps = data_ref.shape[0] // 64
    groups = [(step, half) for step in range(steps) for half in range(2)]
    prepare(*source, *groups[0], buffers[0])
    for index in range(len(groups)):
        if index + 1 < len(groups):
            prepare(*source, *groups[index + 1], buffers[(index + 1) % 8])
        sums = accumulate(buffers[index % 8], sums)
    return sums


def first_kernel(centre_ref, gain_ref, data_ref, even_ref, odd_ref, *scratch):
    zero = jnp.zeros((HALF, P_SIZE), jnp.float32)
    even, odd = sum_blocks(0, centre_ref, gain_ref, data_ref, scratch, (zero, zero))
    even_ref[...] = even
    odd_ref[...] = odd


def last_kernel(
    scale, centre_ref, gain_ref, data_ref, even_ref, odd_ref, keep_ref, send_ref,
    order_ref, *scratch,
):
    even, odd = sum_blocks(
        1, centre_ref, gain_ref, data_ref, scratch, (even_ref[...], odd_ref[...])
    )
    even, odd = even * scale, odd * scale
    core = lax.axis_index("freq") & 1
    far = lax.axis_index("freq") >> 1
    lane = lax.broadcasted_iota(jnp.int32, (8, P_SIZE), 1)
    near = jnp.where((lane & 8) == 8, lane ^ 8, lane ^ 7)
    sign = jnp.where((lane & 8) == 8, -1.0, 1.0)
    for block in range(8):
        base = 16 * (block // 2)
        above = block % 2 == 1
        even_p, even_q = even[base : base + 8], even[base + 8 : base + 16]
        odd_p, odd_q = odd[base : base + 8], odd[base + 8 : base + 16]
        even_row = even_p - even_q if above else even_p + even_q
        odd_row = odd_p + odd_q if above else odd_p - odd_q
        less, more = even_row - odd_row, even_row + odd_row
        for index, one, two, reverse in (
            (8 + block, less, more, not above),
            (7 - block, more, less, above),
        ):
            values = paired(one, near, reverse) + sign * paired(two, near ^ 8, reverse)
            piece = index // 4
            slot = ((piece & 1) ^ core) * 2 + ((piece >> 1) ^ far)
            place = pl.multiple_of(slot * 32 + 8 * (index % 4), 8)
            order_ref[pl.ds(place, 8), :] = values
    keep_ref[...] = order_ref[0:HALF, :]
    send_ref[...] = order_ref[HALF:, :]


SMALL = pltpu.CompilerParams(vmem_limit_bytes=8 << 20)
VMEM = pl.BlockSpec(memory_space=pltpu.VMEM)


def body(total, plane, visibilities, weights, uv_cells, flags, plan, beam, facets):
    arguments = (visibilities, weights, uv_cells, flags, plan[None], beam, facets)
    packed, gains, centre = pl.pallas_call(
        pack_kernel,
        out_shape=(
            jax.ShapeDtypeStruct((plane, 16, LANES), jnp.float32),
            jax.ShapeDtypeStruct((4 * plane, LANES), jnp.float32),
            jax.ShapeDtypeStruct((16, LANES), jnp.int32),
        ),
        in_specs=[pl.BlockSpec(memory_space=pltpu.HBM)] * 7,
        out_specs=(VMEM, VMEM, VMEM),
        scratch_shapes=[pltpu.VMEM(each.shape, each.dtype) for each in arguments]
        + [
            pltpu.VMEM((8, weights.shape[1]), jnp.float32),
            pltpu.SemaphoreType.DMA((len(arguments),)),
        ],
        compiler_params=SMALL,
    )(*(pltpu.with_memory_space_constraint(each, pltpu.HBM) for each in arguments))
    groups = [list(range(side, 2 * plane, 2)) for side in range(2)]
    near = lax.all_to_all(packed, "facet", 0, 0, axis_index_groups=groups)
    near = near.reshape(plane * 16, LANES)
    far = lax.ppermute(near, "facet", [(i, i ^ 1) for i in range(2 * plane)])
    image = jax.ShapeDtypeStruct((HALF, P_SIZE), jnp.float32)
    buffers = [
        pltpu.VMEM((2, 64, LANES), jnp.float32),
        pltpu.VMEM((2, 64, LANES), jnp.float32),
        pltpu.VMEM((16, 8, LANES), jnp.float32),
        pltpu.VMEM((8, 8, LANES), jnp.float32),
    ]
    scratch = buffers * 8
    cost = pl.CostEstimate(
        flops=2 * 2 * HALF * P_SIZE * 2 * plane * KEEP, bytes_accessed=1 << 18, transcendentals=0
    )
    even, odd = pl.pallas_call(
        first_kernel,
        out_shape=(image, image),
        in_specs=[VMEM] * 3,
        out_specs=(VMEM, VMEM),
        scratch_shapes=scratch,
        compiler_params=SMALL,
        cost_estimate=cost,
    )(centre, gains, near)
    keep, send = pl.pallas_call(
        functools.partial(last_kernel, 2.0 / math.sqrt(total)),
        out_shape=(image, image),
        in_specs=[VMEM] * 5,
        out_specs=(VMEM, VMEM),
        scratch_shapes=[pltpu.VMEM((P_SIZE, P_SIZE), jnp.float32)] + scratch,
        compiler_params=SMALL,
        cost_estimate=cost,
    )(centre, gains, far, even, odd)
    half = keep + lax.ppermute(send, "freq", [(i, i ^ 1) for i in range(4)])
    return (half[:32] + lax.ppermute(half[32:], "freq", [(i, i ^ 2) for i in range(4)]))[None]


def solution(mesh):
    in_specs = (
        P("facet", None, "freq"),
        P("facet", "freq"),
        P("facet", None, "freq"),
        P("facet", "freq"),
        P(),
        P("facet", None),
        P("facet", None),
    )
    total = 64 * 2048
    return jax.shard_map(
        functools.partial(body, total, mesh.shape["facet"] // 2),
        mesh=mesh,
        in_specs=in_specs,
        out_specs=P("facet", "freq", None),
        check_vma=False,
    )
```

```python
import functools
import math

import jax
import jax.numpy as jnp
from jax import lax
from jax.experimental import pallas as pl
from jax.experimental.pallas import tpu as pltpu
from jax.sharding import PartitionSpec as P

P_SIZE = 128
IMG = 32768
KEEP = 256
LANES = 128
HALF = P_SIZE // 2


def lane_prefix(flags):
    rows = lax.broadcasted_iota(jnp.int32, (LANES, LANES), 0)
    columns = lax.broadcasted_iota(jnp.int32, (LANES, LANES), 1)
    earlier = (rows < columns).astype(jnp.bfloat16)
    running = jnp.zeros((flags.shape[0], 1), jnp.float32)
    parts = []
    for start in range(0, flags.shape[1], LANES):
        piece = flags[:, start : start + LANES]
        inside = jnp.dot(piece.astype(jnp.bfloat16), earlier, preferred_element_type=jnp.float32)
        parts.append(inside + running)
        running = running + jnp.sum(piece, axis=1, keepdims=True)
    return jnp.concatenate(parts, axis=1)


def pack_kernel(
    vis_in, weight_in, uv_in, flag_in,
    out_ref,
    vis_ref, weight_ref, uv_ref, flag_ref, data_ref, arrived,
):
    copies = [
        pltpu.make_async_copy(source, target, arrived.at[index])
        for index, (source, target) in enumerate(
            (
                (flag_in, flag_ref), (vis_in, vis_ref), (weight_in, weight_ref), (uv_in, uv_ref),
            )
        )
    ]
    for copy in copies:
        copy.start()
    copies[0].wait()
    rows = weight_ref.shape[1]
    flags = flag_ref[...].astype(jnp.float32)
    spot = jnp.where(flags > 0.0, lane_prefix(flags), -1.0).astype(jnp.int32)
    for copy in copies[1:]:
        copy.wait()
    weights = weight_ref[...]
    data_ref[0:2, :] = vis_ref[:, 0, :] * weights
    data_ref[2:4, :] = vis_ref[:, 1, :] * weights
    data_ref[4:6, :] = uv_ref[:, 0, :].astype(jnp.float32)
    data_ref[6:8, :] = uv_ref[:, 1, :].astype(jnp.float32)
    data = data_ref[...]
    high = data.astype(jnp.bfloat16).astype(jnp.float32)
    rest = data - high
    middle = rest.astype(jnp.bfloat16).astype(jnp.float32)
    low = rest - middle
    pieces = jnp.concatenate([high, middle, low], axis=0).astype(jnp.bfloat16)
    target = lax.broadcasted_iota(jnp.int32, (KEEP, rows), 0)
    packed = []
    for block in range(2):
        chosen = (target == spot[block : block + 1, :]).astype(jnp.float32).astype(jnp.bfloat16)
        moved = lax.dot_general(
            pieces, chosen, (((1,), (1,)), ((), ())), preferred_element_type=jnp.float32
        )
        packed.append(moved[0:8] + moved[8:16] + moved[16:24])
    parity = lax.broadcasted_iota(jnp.int32, packed[0].shape, 0) & 1
    result = jnp.where(parity == 0, packed[0], packed[1])
    plane = out_ref.shape[0]
    for peer in range(plane):
        out_ref[peer, 0:8, :] = result[:, :LANES]
        out_ref[peer, 8:16, :] = result[:, LANES:]


def doubled(sine, cosine):
    twice = sine + sine
    return twice * cosine, 1.0 - twice * sine


def sine_cosine(turns):
    x = ((turns << 16) >> 16).astype(jnp.float32) * (2.0 * math.pi / 65536.0 / 4.0)
    y = x * x
    sine = x * (1.0 + y * (-1.0 / 6 + y * (1.0 / 120 + y * (-1.0 / 5040 + y * (1.0 / 362880)))))
    cosine = 1.0 + y * (-0.5 + y * (1.0 / 24 + y * (-1.0 / 720 + y * (1.0 / 40320))))
    return doubled(*doubled(sine, cosine))


def half_steps(sine, cosine, count):
    twice = 4.0 * cosine * cosine - 2.0
    sines, cosines = [sine], [cosine]
    before_sine, before_cosine = -sine, cosine
    for _ in range(count - 1):
        sines.append(twice * sines[-1] - before_sine)
        cosines.append(twice * cosines[-1] - before_cosine)
        before_sine, before_cosine = sines[-2], cosines[-2]
    return sines, cosines


def chunk_tables(outer, fine, count, chunk):
    cosine, sine = fine[0, pl.ds(8 * chunk, 8), :], fine[1, pl.ds(8 * chunk, 8), :]
    first, second = [], []
    for far in range(count):
        x = jnp.broadcast_to(outer[2 * far, pl.ds(chunk, 1), :], (8, LANES))
        y = jnp.broadcast_to(outer[2 * far + 1, pl.ds(chunk, 1), :], (8, LANES))
        first += [x * cosine, y * sine]
        second += [y * cosine, x * sine]
    return (
        jnp.concatenate(first, axis=0).astype(jnp.bfloat16),
        jnp.concatenate(second, axis=0).astype(jnp.bfloat16),
    )


def prepare(which, centre_ref, data_ref, gain_ref, step, half, buffers):
    fine_v, fine_u, outer, coarse = buffers
    column, row = centre_ref[0:8, :], centre_ref[8:16, :]
    tile = step >> 1
    member = step & 1
    owners = gain_ref.shape[0] // 4
    gain = gain_ref[pl.ds(pl.multiple_of((2 * which + member) * owners + tile * 8, 8), 8), :]
    first = tile * 128 + 8 * half + member
    real, imag, u, v = (
        data_ref[pl.ds(first + 2 * kind, 8, stride=16), :] for kind in range(4)
    )
    u = u.astype(jnp.int32)
    v = v.astype(jnp.int32)
    real = real * gain
    imag = imag * gain
    sine, cosine = sine_cosine(u * column + v * row)
    centre_real = real * cosine - imag * sine
    centre_imag = real * sine + imag * cosine
    near_v = sine_cosine(v)
    near_u = sine_cosine(u)
    for near, fine in ((near_v, fine_v), (near_u, fine_u)):
        sines, cosines = half_steps(*near, 8)
        for tau in range(8):
            fine[0, pl.ds(tau, 8, stride=8), :] = cosines[tau]
            fine[1, pl.ds(tau, 8, stride=8), :] = sines[tau]
    for _ in range(4):
        near_v = doubled(*near_v)
        near_u = doubled(*near_u)
    sines, cosines = half_steps(*near_u, 4)
    for far in range(4):
        coarse[2 * far] = cosines[far]
        coarse[2 * far + 1] = sines[far]
    sines, cosines = half_steps(*near_v, 4)
    for far in range(4):
        rc, isn = centre_real * cosines[far], centre_imag * sines[far]
        ic, rs = centre_imag * cosines[far], centre_real * sines[far]
        above, below = 4 + far, 3 - far
        outer[2 * above] = rc - isn
        outer[2 * above + 1] = ic + rs
        outer[2 * below] = rc + isn
        outer[2 * below + 1] = ic - rs


def accumulate(buffers, sums):
    fine_v, fine_u, outer, coarse = buffers
    even, odd = sums
    for pair in range(4):
        tables = [
            chunk_tables(coarse, fine_u, 4, chunk) + chunk_tables(outer, fine_v, 8, chunk)
            for chunk in (2 * pair, 2 * pair + 1)
        ]
        c, s, a, b = (jnp.concatenate(table, axis=1) for table in zip(*tables))
        contract = (((1,), (1,)), ((), ()))
        even = even + lax.dot_general(c, a, contract, preferred_element_type=jnp.float32)
        odd = odd + lax.dot_general(s, b, contract, preferred_element_type=jnp.float32)
    return even, odd


def paired(values, source, reverse):
    values = jnp.take_along_axis(values, source, axis=1)
    if reverse:
        values = jnp.take_along_axis(
            values, 7 - lax.broadcasted_iota(jnp.int32, values.shape, 0), axis=0
        )
    return values


def sum_blocks(which, centre_ref, gain_ref, data_ref, scratch, sums):
    buffers = [scratch[4 * k : 4 * k + 4] for k in range(8)]
    source = (which, centre_ref, data_ref, gain_ref)
    steps = data_ref.shape[0] // 64
    groups = [(step, half) for step in range(steps) for half in range(2)]
    prepare(*source, *groups[0], buffers[0])
    for index in range(len(groups)):
        if index + 1 < len(groups):
            prepare(*source, *groups[index + 1], buffers[(index + 1) % 8])
        sums = accumulate(buffers[index % 8], sums)
    return sums


def first_kernel(
    plan_in, beam_in, facet_in, data_ref, even_ref, odd_ref, gain_ref, centre_ref,
    plan_ref, beam_ref, facet_ref, arrived, *scratch,
):
    copies = [
        pltpu.make_async_copy(source, target, arrived.at[index])
        for index, (source, target) in enumerate(
            ((plan_in, plan_ref), (beam_in, beam_ref), (facet_in, facet_ref))
        )
    ]
    for copy in copies:
        copy.start()
    for copy in copies:
        copy.wait()
    plane = gain_ref.shape[0] // 4
    side = lax.axis_index("facet") & 1
    shape = (plane, plan_ref.shape[1])
    for which in range(2):
        for member in range(2):
            block = 4 * lax.broadcasted_iota(jnp.int32, shape, 0) + 2 * (side ^ which) + member
            matches = plan_ref[...] == block
            gain = jnp.sum(jnp.where(matches, beam_ref[...], 0.0), axis=1, keepdims=True)
            first = (2 * which + member) * plane
            gain_ref[first : first + plane, :] = jnp.broadcast_to(gain, (plane, LANES))
    for axis in range(2):
        centre = 2 * (facet_ref[0:1, axis : axis + 1] * P_SIZE - IMG // 2) + (P_SIZE - 1)
        centre_ref[8 * axis : 8 * axis + 8, :] = jnp.broadcast_to(centre, (8, LANES))
    zero = jnp.zeros((HALF, P_SIZE), jnp.float32)
    even, odd = sum_blocks(0, centre_ref, gain_ref, data_ref, scratch, (zero, zero))
    even_ref[...] = even
    odd_ref[...] = odd


def last_kernel(
    scale, centre_ref, gain_ref, data_ref, even_ref, odd_ref, keep_ref, send_ref,
    order_ref, *scratch,
):
    even, odd = sum_blocks(
        1, centre_ref, gain_ref, data_ref, scratch, (even_ref[...], odd_ref[...])
    )
    even, odd = even * scale, odd * scale
    core = lax.axis_index("freq") & 1
    far = lax.axis_index("freq") >> 1
    lane = lax.broadcasted_iota(jnp.int32, (8, P_SIZE), 1)
    near = jnp.where((lane & 8) == 8, lane ^ 8, lane ^ 7)
    sign = jnp.where((lane & 8) == 8, -1.0, 1.0)
    for block in range(8):
        base = 16 * (block // 2)
        above = block % 2 == 1
        even_p, even_q = even[base : base + 8], even[base + 8 : base + 16]
        odd_p, odd_q = odd[base : base + 8], odd[base + 8 : base + 16]
        even_row = even_p - even_q if above else even_p + even_q
        odd_row = odd_p + odd_q if above else odd_p - odd_q
        less, more = even_row - odd_row, even_row + odd_row
        for index, one, two, reverse in (
            (8 + block, less, more, not above),
            (7 - block, more, less, above),
        ):
            values = paired(one, near, reverse) + sign * paired(two, near ^ 8, reverse)
            piece = index // 4
            slot = ((piece & 1) ^ core) * 2 + ((piece >> 1) ^ far)
            place = pl.multiple_of(slot * 32 + 8 * (index % 4), 8)
            order_ref[pl.ds(place, 8), :] = values
    keep_ref[...] = order_ref[0:HALF, :]
    send_ref[...] = order_ref[HALF:, :]


SMALL = pltpu.CompilerParams(vmem_limit_bytes=8 << 20)
VMEM = pl.BlockSpec(memory_space=pltpu.VMEM)


def body(total, plane, visibilities, weights, uv_cells, flags, plan, beam, facets):
    def in_hbm(*arrays):
        return [pltpu.with_memory_space_constraint(each, pltpu.HBM) for each in arrays]

    arguments = (visibilities, weights, uv_cells, flags)
    packed = pl.pallas_call(
        pack_kernel,
        out_shape=jax.ShapeDtypeStruct((plane, 16, LANES), jnp.float32),
        in_specs=[pl.BlockSpec(memory_space=pltpu.HBM)] * 4,
        out_specs=VMEM,
        scratch_shapes=[pltpu.VMEM(each.shape, each.dtype) for each in arguments]
        + [
            pltpu.VMEM((8, weights.shape[1]), jnp.float32),
            pltpu.SemaphoreType.DMA((len(arguments),)),
        ],
        compiler_params=SMALL,
    )(*in_hbm(*arguments))
    notes = (plan[None], beam, facets)
    groups = [list(range(side, 2 * plane, 2)) for side in range(2)]
    near = lax.all_to_all(packed, "facet", 0, 0, axis_index_groups=groups)
    near = near.reshape(plane * 16, LANES)
    far = lax.ppermute(near, "facet", [(i, i ^ 1) for i in range(2 * plane)])
    image = jax.ShapeDtypeStruct((HALF, P_SIZE), jnp.float32)
    buffers = [
        pltpu.VMEM((2, 64, LANES), jnp.float32),
        pltpu.VMEM((2, 64, LANES), jnp.float32),
        pltpu.VMEM((16, 8, LANES), jnp.float32),
        pltpu.VMEM((8, 8, LANES), jnp.float32),
    ]
    scratch = buffers * 8
    cost = pl.CostEstimate(
        flops=2 * 2 * HALF * P_SIZE * 2 * plane * KEEP, bytes_accessed=1 << 18, transcendentals=0
    )
    even, odd, gains, centre = pl.pallas_call(
        first_kernel,
        out_shape=(
            image,
            image,
            jax.ShapeDtypeStruct((4 * plane, LANES), jnp.float32),
            jax.ShapeDtypeStruct((16, LANES), jnp.int32),
        ),
        in_specs=[pl.BlockSpec(memory_space=pltpu.HBM)] * 3 + [VMEM],
        out_specs=(VMEM,) * 4,
        scratch_shapes=[pltpu.VMEM(each.shape, each.dtype) for each in notes]
        + [pltpu.SemaphoreType.DMA((3,))]
        + scratch,
        compiler_params=SMALL,
        cost_estimate=cost,
    )(*in_hbm(*notes), near)
    keep, send = pl.pallas_call(
        functools.partial(last_kernel, 2.0 / math.sqrt(total)),
        out_shape=(image, image),
        in_specs=[VMEM] * 5,
        out_specs=(VMEM, VMEM),
        scratch_shapes=[pltpu.VMEM((P_SIZE, P_SIZE), jnp.float32)] + scratch,
        compiler_params=SMALL,
        cost_estimate=cost,
    )(centre, gains, far, even, odd)
    half = keep + lax.ppermute(send, "freq", [(i, i ^ 1) for i in range(4)])
    return (half[:32] + lax.ppermute(half[32:], "freq", [(i, i ^ 2) for i in range(4)]))[None]


def solution(mesh):
    in_specs = (
        P("facet", None, "freq"),
        P("facet", "freq"),
        P("facet", None, "freq"),
        P("facet", "freq"),
        P(),
        P("facet", None),
        P("facet", None),
    )
    total = 64 * 2048
    return jax.shard_map(
        functools.partial(body, total, mesh.shape["facet"] // 2),
        mesh=mesh,
        in_specs=in_specs,
        out_specs=P("facet", "freq", None),
        check_vma=False,
    )
```

```python
import functools
import math

import jax
import jax.numpy as jnp
from jax import lax
from jax.experimental import pallas as pl
from jax.experimental.pallas import tpu as pltpu
from jax.sharding import PartitionSpec as P

P_SIZE = 128
IMG = 32768
KEEP = 256
LANES = 128
HALF = P_SIZE // 2


def lane_prefix(flags):
    rows = lax.broadcasted_iota(jnp.int32, (LANES, LANES), 0)
    columns = lax.broadcasted_iota(jnp.int32, (LANES, LANES), 1)
    earlier = (rows < columns).astype(jnp.bfloat16)
    count = flags.shape[0]
    pieces = [flags[:, start : start + LANES] for start in range(0, flags.shape[1], LANES)]
    stacked = jnp.concatenate(pieces, axis=0)
    inside = jnp.dot(stacked.astype(jnp.bfloat16), earlier, preferred_element_type=jnp.float32)
    running = jnp.zeros((count, 1), jnp.float32)
    parts = []
    for index, piece in enumerate(pieces):
        parts.append(inside[index * count : (index + 1) * count] + running)
        running = running + jnp.sum(piece, axis=1, keepdims=True)
    return jnp.concatenate(parts, axis=1)


def pack_kernel(
    vis_in, weight_in, uv_in, flag_in,
    out_ref,
    vis_ref, weight_ref, uv_ref, flag_ref, data_ref, arrived,
):
    copies = [
        pltpu.make_async_copy(source, target, arrived.at[index])
        for index, (source, target) in enumerate(
            (
                (flag_in, flag_ref), (vis_in, vis_ref), (weight_in, weight_ref), (uv_in, uv_ref),
            )
        )
    ]
    for copy in copies:
        copy.start()
    copies[0].wait()
    rows = weight_ref.shape[1]
    flags = flag_ref[...].astype(jnp.float32)
    spot = jnp.where(flags > 0.0, lane_prefix(flags), -1.0).astype(jnp.int32)
    for copy in copies[1:]:
        copy.wait()
    weights = weight_ref[...]
    data_ref[0:2, :] = vis_ref[:, 0, :] * weights
    data_ref[2:4, :] = vis_ref[:, 1, :] * weights
    data_ref[4:6, :] = uv_ref[:, 0, :].astype(jnp.float32)
    data_ref[6:8, :] = uv_ref[:, 1, :].astype(jnp.float32)
    data = data_ref[...]
    high = data.astype(jnp.bfloat16).astype(jnp.float32)
    rest = data - high
    middle = rest.astype(jnp.bfloat16).astype(jnp.float32)
    low = rest - middle
    pieces = jnp.concatenate([high, middle, low], axis=0).astype(jnp.bfloat16)
    target = lax.broadcasted_iota(jnp.int32, (KEEP, rows), 0)
    packed = []
    for block in range(2):
        chosen = (target == spot[block : block + 1, :]).astype(jnp.float32).astype(jnp.bfloat16)
        moved = lax.dot_general(
            pieces, chosen, (((1,), (1,)), ((), ())), preferred_element_type=jnp.float32
        )
        packed.append(moved[0:8] + moved[8:16] + moved[16:24])
    parity = lax.broadcasted_iota(jnp.int32, packed[0].shape, 0) & 1
    result = jnp.where(parity == 0, packed[0], packed[1])
    plane = out_ref.shape[0]
    for peer in range(plane):
        out_ref[peer, 0:8, :] = result[:, :LANES]
        out_ref[peer, 8:16, :] = result[:, LANES:]


def doubled(sine, cosine):
    twice = sine + sine
    return twice * cosine, 1.0 - twice * sine


def sine_cosine(turns):
    x = ((turns << 16) >> 16).astype(jnp.float32) * (2.0 * math.pi / 65536.0 / 4.0)
    y = x * x
    sine = x * (1.0 + y * (-1.0 / 6 + y * (1.0 / 120 + y * (-1.0 / 5040 + y * (1.0 / 362880)))))
    cosine = 1.0 + y * (-0.5 + y * (1.0 / 24 + y * (-1.0 / 720 + y * (1.0 / 40320))))
    return doubled(*doubled(sine, cosine))


def half_steps(sine, cosine, count):
    twice = 4.0 * cosine * cosine - 2.0
    sines, cosines = [sine], [cosine]
    before_sine, before_cosine = -sine, cosine
    for _ in range(count - 1):
        sines.append(twice * sines[-1] - before_sine)
        cosines.append(twice * cosines[-1] - before_cosine)
        before_sine, before_cosine = sines[-2], cosines[-2]
    return sines, cosines


def chunk_tables(outer, fine, count, chunk):
    cosine, sine = fine[0, pl.ds(8 * chunk, 8), :], fine[1, pl.ds(8 * chunk, 8), :]
    first, second = [], []
    for far in range(count):
        x = jnp.broadcast_to(outer[2 * far, pl.ds(chunk, 1), :], (8, LANES))
        y = jnp.broadcast_to(outer[2 * far + 1, pl.ds(chunk, 1), :], (8, LANES))
        first += [x * cosine, y * sine]
        second += [y * cosine, x * sine]
    return (
        jnp.concatenate(first, axis=0).astype(jnp.bfloat16),
        jnp.concatenate(second, axis=0).astype(jnp.bfloat16),
    )


def prepare(which, centre_ref, data_ref, gain_ref, step, half, buffers):
    fine_v, fine_u, outer, coarse = buffers
    column, row = centre_ref[0:8, :], centre_ref[8:16, :]
    tile = step >> 1
    member = step & 1
    owners = gain_ref.shape[0] // 4
    gain = gain_ref[pl.ds(pl.multiple_of((2 * which + member) * owners + tile * 8, 8), 8), :]
    first = tile * 128 + 8 * half + member
    real, imag, u, v = (
        data_ref[pl.ds(first + 2 * kind, 8, stride=16), :] for kind in range(4)
    )
    u = u.astype(jnp.int32)
    v = v.astype(jnp.int32)
    real = real * gain
    imag = imag * gain
    sine, cosine = sine_cosine(u * column + v * row)
    centre_real = real * cosine - imag * sine
    centre_imag = real * sine + imag * cosine
    near_v = sine_cosine(v)
    near_u = sine_cosine(u)
    for near, fine in ((near_v, fine_v), (near_u, fine_u)):
        sines, cosines = half_steps(*near, 8)
        for tau in range(8):
            fine[0, pl.ds(tau, 8, stride=8), :] = cosines[tau]
            fine[1, pl.ds(tau, 8, stride=8), :] = sines[tau]
    for _ in range(4):
        near_v = doubled(*near_v)
        near_u = doubled(*near_u)
    sines, cosines = half_steps(*near_u, 4)
    for far in range(4):
        coarse[2 * far] = cosines[far]
        coarse[2 * far + 1] = sines[far]
    sines, cosines = half_steps(*near_v, 4)
    for far in range(4):
        rc, isn = centre_real * cosines[far], centre_imag * sines[far]
        ic, rs = centre_imag * cosines[far], centre_real * sines[far]
        above, below = 4 + far, 3 - far
        outer[2 * above] = rc - isn
        outer[2 * above + 1] = ic + rs
        outer[2 * below] = rc + isn
        outer[2 * below + 1] = ic - rs


def accumulate(buffers, sums):
    fine_v, fine_u, outer, coarse = buffers
    even, odd = sums
    for pair in range(4):
        tables = [
            chunk_tables(coarse, fine_u, 4, chunk) + chunk_tables(outer, fine_v, 8, chunk)
            for chunk in (2 * pair, 2 * pair + 1)
        ]
        c, s, a, b = (jnp.concatenate(table, axis=1) for table in zip(*tables))
        contract = (((1,), (1,)), ((), ()))
        even = even + lax.dot_general(c, a, contract, preferred_element_type=jnp.float32)
        odd = odd + lax.dot_general(s, b, contract, preferred_element_type=jnp.float32)
    return even, odd


def paired(values, source, reverse):
    values = jnp.take_along_axis(values, source, axis=1)
    if reverse:
        values = jnp.take_along_axis(
            values, 7 - lax.broadcasted_iota(jnp.int32, values.shape, 0), axis=0
        )
    return values


def sum_blocks(which, centre_ref, gain_ref, data_ref, scratch, sums):
    buffers = [scratch[4 * k : 4 * k + 4] for k in range(8)]
    source = (which, centre_ref, data_ref, gain_ref)
    steps = data_ref.shape[0] // 64
    groups = [(step, half) for step in range(steps) for half in range(2)]
    prepare(*source, *groups[0], buffers[0])
    for index in range(len(groups)):
        if index + 1 < len(groups):
            prepare(*source, *groups[index + 1], buffers[(index + 1) % 8])
        sums = accumulate(buffers[index % 8], sums)
    return sums


def first_kernel(
    plan_in, beam_in, facet_in, data_ref, even_ref, odd_ref, gain_ref, centre_ref,
    plan_ref, beam_ref, facet_ref, arrived, *scratch,
):
    copies = [
        pltpu.make_async_copy(source, target, arrived.at[index])
        for index, (source, target) in enumerate(
            ((plan_in, plan_ref), (beam_in, beam_ref), (facet_in, facet_ref))
        )
    ]
    for copy in copies:
        copy.start()
    for copy in copies:
        copy.wait()
    plane = gain_ref.shape[0] // 4
    side = lax.axis_index("facet") & 1
    shape = (plane, plan_ref.shape[1])
    for which in range(2):
        for member in range(2):
            block = 4 * lax.broadcasted_iota(jnp.int32, shape, 0) + 2 * (side ^ which) + member
            matches = plan_ref[...] == block
            gain = jnp.sum(jnp.where(matches, beam_ref[...], 0.0), axis=1, keepdims=True)
            first = (2 * which + member) * plane
            gain_ref[first : first + plane, :] = jnp.broadcast_to(gain, (plane, LANES))
    for axis in range(2):
        centre = 2 * (facet_ref[0:1, axis : axis + 1] * P_SIZE - IMG // 2) + (P_SIZE - 1)
        centre_ref[8 * axis : 8 * axis + 8, :] = jnp.broadcast_to(centre, (8, LANES))
    zero = jnp.zeros((HALF, P_SIZE), jnp.float32)
    even, odd = sum_blocks(0, centre_ref, gain_ref, data_ref, scratch, (zero, zero))
    even_ref[...] = even
    odd_ref[...] = odd


def last_kernel(
    scale, centre_ref, gain_ref, data_ref, even_ref, odd_ref, keep_ref, send_ref,
    order_ref, *scratch,
):
    even, odd = sum_blocks(
        1, centre_ref, gain_ref, data_ref, scratch, (even_ref[...], odd_ref[...])
    )
    even, odd = even * scale, odd * scale
    core = lax.axis_index("freq") & 1
    far = lax.axis_index("freq") >> 1
    lane = lax.broadcasted_iota(jnp.int32, (8, P_SIZE), 1)
    near = jnp.where((lane & 8) == 8, lane ^ 8, lane ^ 7)
    sign = jnp.where((lane & 8) == 8, -1.0, 1.0)
    for block in range(8):
        base = 16 * (block // 2)
        above = block % 2 == 1
        even_p, even_q = even[base : base + 8], even[base + 8 : base + 16]
        odd_p, odd_q = odd[base : base + 8], odd[base + 8 : base + 16]
        even_row = even_p - even_q if above else even_p + even_q
        odd_row = odd_p + odd_q if above else odd_p - odd_q
        less, more = even_row - odd_row, even_row + odd_row
        for index, one, two, reverse in (
            (8 + block, less, more, not above),
            (7 - block, more, less, above),
        ):
            values = paired(one, near, reverse) + sign * paired(two, near ^ 8, reverse)
            piece = index // 4
            slot = ((piece & 1) ^ core) * 2 + ((piece >> 1) ^ far)
            place = pl.multiple_of(slot * 32 + 8 * (index % 4), 8)
            order_ref[pl.ds(place, 8), :] = values
    keep_ref[...] = order_ref[0:HALF, :]
    send_ref[...] = order_ref[HALF:, :]


SMALL = pltpu.CompilerParams(vmem_limit_bytes=8 << 20)
VMEM = pl.BlockSpec(memory_space=pltpu.VMEM)


def body(total, plane, visibilities, weights, uv_cells, flags, plan, beam, facets):
    def in_hbm(*arrays):
        return [pltpu.with_memory_space_constraint(each, pltpu.HBM) for each in arrays]

    arguments = (visibilities, weights, uv_cells, flags)
    packed = pl.pallas_call(
        pack_kernel,
        out_shape=jax.ShapeDtypeStruct((plane, 16, LANES), jnp.float32),
        in_specs=[pl.BlockSpec(memory_space=pltpu.HBM)] * 4,
        out_specs=VMEM,
        scratch_shapes=[pltpu.VMEM(each.shape, each.dtype) for each in arguments]
        + [
            pltpu.VMEM((8, weights.shape[1]), jnp.float32),
            pltpu.SemaphoreType.DMA((len(arguments),)),
        ],
        compiler_params=SMALL,
    )(*in_hbm(*arguments))
    notes = (plan[None], beam, facets)
    groups = [list(range(side, 2 * plane, 2)) for side in range(2)]
    near = lax.all_to_all(packed, "facet", 0, 0, axis_index_groups=groups)
    near = near.reshape(plane * 16, LANES)
    far = lax.ppermute(near, "facet", [(i, i ^ 1) for i in range(2 * plane)])
    image = jax.ShapeDtypeStruct((HALF, P_SIZE), jnp.float32)
    buffers = [
        pltpu.VMEM((2, 64, LANES), jnp.float32),
        pltpu.VMEM((2, 64, LANES), jnp.float32),
        pltpu.VMEM((16, 8, LANES), jnp.float32),
        pltpu.VMEM((8, 8, LANES), jnp.float32),
    ]
    scratch = buffers * 8
    cost = pl.CostEstimate(
        flops=2 * 2 * HALF * P_SIZE * 2 * plane * KEEP, bytes_accessed=1 << 18, transcendentals=0
    )
    even, odd, gains, centre = pl.pallas_call(
        first_kernel,
        out_shape=(
            image,
            image,
            jax.ShapeDtypeStruct((4 * plane, LANES), jnp.float32),
            jax.ShapeDtypeStruct((16, LANES), jnp.int32),
        ),
        in_specs=[pl.BlockSpec(memory_space=pltpu.HBM)] * 3 + [VMEM],
        out_specs=(VMEM,) * 4,
        scratch_shapes=[pltpu.VMEM(each.shape, each.dtype) for each in notes]
        + [pltpu.SemaphoreType.DMA((3,))]
        + scratch,
        compiler_params=SMALL,
        cost_estimate=cost,
    )(*in_hbm(*notes), near)
    keep, send = pl.pallas_call(
        functools.partial(last_kernel, 2.0 / math.sqrt(total)),
        out_shape=(image, image),
        in_specs=[VMEM] * 5,
        out_specs=(VMEM, VMEM),
        scratch_shapes=[pltpu.VMEM((P_SIZE, P_SIZE), jnp.float32)] + scratch,
        compiler_params=SMALL,
        cost_estimate=cost,
    )(centre, gains, far, even, odd)
    half = keep + lax.ppermute(send, "freq", [(i, i ^ 1) for i in range(4)])
    return (half[:32] + lax.ppermute(half[32:], "freq", [(i, i ^ 2) for i in range(4)]))[None]


def solution(mesh):
    in_specs = (
        P("facet", None, "freq"),
        P("facet", "freq"),
        P("facet", None, "freq"),
        P("facet", "freq"),
        P(),
        P("facet", None),
        P("facet", None),
    )
    total = 64 * 2048
    return jax.shard_map(
        functools.partial(body, total, mesh.shape["facet"] // 2),
        mesh=mesh,
        in_specs=in_specs,
        out_specs=P("facet", "freq", None),
        check_vma=False,
    )
```
